256 devices in a mesh: clip: 16 (over x, z_hi), seq: 16 (over y, z_lo, core).
Axes of the slice: x: 4, y: 4, z: 8 (z_hi: 4, z_lo: 2; z = z_hi * 2 + z_lo), core: 2. Of those that a mesh axis runs over, the one named last changes fastest.
Arguments:
- tokens: bfloat16 [16, 8192, 768], P('clip', 'seq'), may hold values from -6 to 6
- out_grad: bfloat16 [16, 8192, 768], P('clip', 'seq'), may hold values from -6144 to 6144
- saved_logits: bfloat16 [16, 8192, 1024], P('clip', 'seq'), may hold values from -14 to 400
- slot_params: bfloat16 [768, 1024], P(None, 'seq'), may hold values from -0.21875 to 0.21875
- slot_inputs: bfloat16 [16, 1024, 768], P(None, ('clip', 'seq')), may hold values from -6 to 6
- slot_outputs: bfloat16 [16, 1024, 768], P('clip', 'seq'), may hold values from -0.119628906 to 0.119628906
- expert_in: bfloat16 [256, 768, 3072], P(('clip', 'seq')), may hold values from -0.21875 to 0.21875
- expert_out: bfloat16 [256, 3072, 768], P(('clip', 'seq')), may hold values from -0.109375 to 0.109375
Outputs:
- token_grad: bfloat16 [16, 8192, 768], P('clip', 'seq')
The draws below stay inside these ranges and needn't reach their ends.
All inputs are finite; a program needn't handle non-finite values.
Results may differ from the reference program's by a relative error of at most 0.023.
Values may be sent and summed in bfloat16 or wider, within the bound.
A program may use at most 64 MiB of HBM per device.

```python
import math
import jax
import jax.numpy as jnp
from jax import lax

D = 768
HID = 3072
SLOTS = 4
EXPERTS = 256
CLIPS = 16
LENGTH = 8192
SLOTS_CLIP = 1024


def draw_saved_logits(key, part):
    keys = jax.random.split(jax.random.fold_in(key, 7), 3)
    position = jnp.arange(LENGTH, dtype=jnp.float32) / LENGTH
    shape = (CLIPS, LENGTH, SLOTS_CLIP)
    noise_draw = jnp.clip(jax.random.normal(keys[0], shape, jnp.float32), -4.0, 4.0)
    row_scale = jnp.exp(jax.random.uniform(keys[1], (CLIPS, LENGTH, 1), jnp.float32, math.log(0.5), math.log(2.0)))
    col_scale = jnp.exp(jax.random.uniform(keys[2], (CLIPS, 1, SLOTS_CLIP), jnp.float32, math.log(0.95), math.log(1.05)))
    ramp_term = math.log(3.0) * position
    return (noise_draw * row_scale * col_scale + ramp_term[None, :, None]).astype(jnp.bfloat16)


def block_levels(key, dims, cuts, smallest, top_value):
    loudness, own = 1.0, jax.random.fold_in(key, 6)
    for dim, shards_of in cuts:
        draws = jnp.exp(jax.random.uniform(jax.random.fold_in(own, dim), (shards_of,), jnp.float32, smallest / len(cuts), top_value / len(cuts)))
        loudness = loudness * jnp.repeat(draws, dims[dim] // shards_of).reshape([-1 if axis == dim else 1 for axis in range(len(dims))])
    return loudness


def gaussian(key, extent, scale, most, cuts=(), kind=jnp.bfloat16):
    level = block_levels(key, extent, cuts, -0.22, 0.18) if cuts else 1.0
    drawn = jax.random.normal(key, extent, jnp.float32) * scale * level
    return jnp.minimum(jnp.maximum(drawn, -most), most).astype(kind)


def setup_inputs(seed: int = 0) -> dict:
    key_list = jax.random.split(jax.random.key(seed), 9)
    return {
        "tokens": gaussian(key_list[0], (CLIPS, LENGTH, D), 1.0, 6.0, ((0, 16), (1, 16))),
        "out_grad": gaussian(key_list[1], (CLIPS, LENGTH, D), 1024.0, 6144.0, ((0, 16), (1, 16))),
        "saved_logits": draw_saved_logits(jax.random.fold_in(key_list[8], 71), 0),
        "slot_params": gaussian(key_list[3], (D, SLOTS_CLIP), D ** -0.5, 0.21875, ((1, 16),)),
        "slot_inputs": gaussian(key_list[4], (CLIPS, SLOTS_CLIP, D), 1.0, 6.0, ((1, 256),)),
        "slot_outputs": gaussian(key_list[5], (CLIPS, SLOTS_CLIP, D), 0.02, 0.119628906, ((0, 16), (1, 16))),
        "expert_in": gaussian(key_list[6], (EXPERTS, D, HID), D ** -0.5, 0.21875, ((0, 256),)),
        "expert_out": gaussian(key_list[7], (EXPERTS, HID, D), HID ** -0.5, 0.109375, ((0, 256),)),
    }


def softmax_pair(logit_raw):
    scores = logit_raw.astype(jnp.float32)
    combine = jax.nn.softmax(scores, axis=1)
    dispatch = jax.nn.softmax(scores, axis=0)
    return (combine, dispatch)

def combine_part(combine, out_cot, slot_out):
    comb_cot = jnp.dot(out_cot, slot_out.T, preferred_element_type=jnp.float32)
    return combine * (comb_cot - lax.optimization_barrier(jnp.sum(combine * comb_cot, axis=1, keepdims=True)))

def front_pass(operands):
    logit_raw, out_cot = operands
    combine, dispatch = softmax_pair(logit_raw)
    return jnp.dot(combine.astype(jnp.bfloat16).T, out_cot, preferred_element_type=jnp.float32).astype(jnp.bfloat16)

def expert_grad(operands):
    slot_in, slot_cot, weight_in, weight_out = operands
    hidden = jnp.dot(slot_in, weight_in, preferred_element_type=jnp.float32)
    act_cot = jnp.dot(slot_cot, weight_out.T, preferred_element_type=jnp.float32)
    unused, pull_back = jax.vjp(jax.nn.gelu, hidden)
    hidden_cot = pull_back(act_cot)[0].astype(jnp.bfloat16)
    return jnp.dot(hidden_cot, weight_in.T, preferred_element_type=jnp.float32).astype(jnp.bfloat16)

def reference(tokens, out_grad, saved_logits, slot_params, slot_inputs, slot_outputs, expert_in, expert_out):
    slot_cot = lax.map(front_pass, (saved_logits, out_grad))
    stacked_in = slot_inputs.reshape(CLIPS, EXPERTS, SLOTS, D).transpose(1, 0, 2, 3).reshape(EXPERTS, CLIPS * SLOTS, D)
    stacked_cot = slot_cot.reshape(CLIPS, EXPERTS, SLOTS, D).transpose(1, 0, 2, 3).reshape(EXPERTS, CLIPS * SLOTS, D)
    stacked_grad = lax.map(expert_grad, (stacked_in, stacked_cot, expert_in, expert_out))
    slot_grad = stacked_grad.reshape(EXPERTS, CLIPS, SLOTS, D).transpose(1, 0, 2, 3).reshape(CLIPS, EXPERTS * SLOTS, D)

    def back_pass(operands):
        tok_feats, out_cot, logit_raw, slot_out, grads = operands
        combine, dispatch = softmax_pair(logit_raw)
        comb_logit = combine_part(combine, out_cot, slot_out)
        disp_cot = jnp.dot(tok_feats, grads.T, preferred_element_type=jnp.float32)
        col_sums = lax.optimization_barrier(jnp.sum(dispatch * disp_cot, axis=0, keepdims=True))
        disp_logit = dispatch * (disp_cot - col_sums)
        logit_grad = (comb_logit + disp_logit).astype(jnp.bfloat16)
        direct = jnp.dot(dispatch.astype(jnp.bfloat16), grads, preferred_element_type=jnp.float32)
        through = jnp.dot(logit_grad, slot_params.T, preferred_element_type=jnp.float32)
        return (direct + through).astype(jnp.bfloat16)
    return lax.map(back_pass, (tokens, out_grad, saved_logits, slot_outputs, slot_grad))
```

```python
import jax
import jax.numpy as jnp
from jax import lax
from jax.experimental import pallas as pl
from jax.experimental.pallas import tpu as pltpu
from jax.sharding import PartitionSpec as P

F32 = jnp.float32
BF16 = jnp.bfloat16
MESH = pl.DeviceIdType.MESH
NT = (((1,), (1,)), ((), ()))
TN = (((0,), (0,)), ((), ()))


def gelu_slope(x):
    k = 0.7978845608028654
    t = jnp.tanh(k * (x + 0.044715 * x * x * x))
    return 0.5 * (1.0 + t) + 0.5 * x * (1.0 - t * t) * (k * (1.0 + 0.134145 * x * x))


def kernel(
    tok_h, og_h, lg_h, pt_h, xin_h, so_h, win_h, wout_h, out_ref,
    lg, og, tok, win, wout, xin, cf, cb, pb, rp, hb, ry, st, qf, a2s, a2r, xf, gp, b2s, b2r, zf, sgb,
    ob, ptb, cc, ddf, dspf, dspb, stl, stb, dtl, dtb, acc,
    ld, cs_s, cs_r, y_s, y_r, a_s, a_r, b_s, b_r, g_s, g_r, k_s, k_r, o_s, o_r, p_s, p_r, st_s, st_r, dt_s, dt_r,
):
    c = lax.axis_index("clip")
    s = lax.axis_index("seq")
    y, q, h = s // 4, s % 4, s % 2
    zl = q // 2
    yr, y2, yl = (y + 1) % 4, (y + 2) % 4, (y + 3) % 4
    right, left = (c, yr * 4 + q), (c, yl * 4 + q)
    mate = (c, s + 1 - 2 * h)
    zmate = (c, s + 2 - 4 * zl)
    mine = pl.ds(pl.multiple_of(h * 384, 128), 384)
    other = pl.ds(pl.multiple_of((1 - h) * 384, 128), 384)

    def rows_of(yy):
        return pl.ds(pl.multiple_of(yy * 16, 16), 16)

    def remote(src, dst, ssem, rsem, dev):
        return pltpu.make_async_remote_copy(
            src_ref=src, dst_ref=dst, send_sem=ssem, recv_sem=rsem, device_id=dev, device_id_type=MESH
        )

    def plane(i):
        return ((c + i // 4) % 16, y * 4 + (q + i % 4) % 4)

    def group(i):
        return (c, (s + i) % 16)

    loads = [
        pltpu.make_async_copy(lg_h.at[0], lg, ld.at[0]),
        pltpu.make_async_copy(og_h.at[0], og, ld.at[1]),
        pltpu.make_async_copy(so_h.at[0], ob.at[y, zl, h], ld.at[2]),
        pltpu.make_async_copy(pt_h, ptb.at[y, zl, h], ld.at[3]),
        pltpu.make_async_copy(xin_h, xin, ld.at[4]),
        pltpu.make_async_copy(win_h.at[0], win, ld.at[5]),
        pltpu.make_async_copy(wout_h.at[0], wout, ld.at[6]),
        pltpu.make_async_copy(tok_h.at[0], tok, ld.at[7]),
    ]
    for load in loads:
        load.start()

    barrier = pltpu.get_barrier_semaphore()

    def greet_plane(i, carry):
        pl.semaphore_signal(barrier, inc=1, device_id=plane(i), device_id_type=MESH)
        return carry

    def greet_group(i, carry):
        pl.semaphore_signal(
            barrier, inc=1, device_id=(c, ((y + 1 + i // 4) % 4) * 4 + i % 4), device_id_type=MESH
        )
        return carry

    lax.fori_loop(0, 12, greet_group, 0)
    lax.fori_loop(1, 64, greet_plane, 0)

    loads[0].wait()

    def front(i, carry):
        rows = pl.ds(pl.multiple_of(i * 64, 64), 64)
        l = lg[rows, :].astype(F32)
        e = jnp.exp(l - jnp.max(l, axis=1, keepdims=True))
        comb = e * (1.0 / jnp.sum(e, axis=1, keepdims=True))
        cf[rows, :] = comb
        cb[rows, :] = comb.astype(BF16)
        return carry

    lax.fori_loop(0, 8, front, 0)
    loads[1].wait()
    pl.semaphore_wait(barrier, 75)

    def cs_copy(k):
        part = pl.ds(k * 4, 4)
        return remote(pb.at[part, :, other], rp.at[part], cs_s.at[k], cs_r.at[k], mate)

    def partial(k, carry):
        cols = pl.ds(pl.multiple_of(k * 256, 256), 256)
        p = lax.dot_general(cb[:, cols], og[...], TN, preferred_element_type=F32)
        pb[pl.ds(k * 4, 4)] = p.astype(BF16).reshape(4, 64, 768)
        cs_copy(k).start()
        return carry

    lax.fori_loop(0, 4, partial, 0)

    loads[2].wait()
    loads[3].wait()
    z_o = remote(ob.at[y, zl, h], ob.at[y, zl, h], o_s.at[0], o_r.at[0], zmate)
    z_p = remote(ptb.at[y, zl, h], ptb.at[y, zl, h], p_s.at[0], p_r.at[0], zmate)
    z_o.start()
    z_p.start()

    def half_sum(k, carry):
        part = pl.ds(k * 4, 4)
        cs_copy(k).wait_recv()
        hb[part] = (pb[part, :, mine].astype(F32) + rp[part].astype(F32)).astype(BF16)
        return carry

    lax.fori_loop(0, 4, half_sum, 0)

    A, B = pl.ds(0, 8), pl.ds(8, 8)

    def y_copy(i, src, dev):
        return remote(src, ry.at[i], y_s.at[i], y_r.at[i], dev)

    ys = [
        y_copy(0, hb.at[A, rows_of(y2)], right),
        y_copy(1, hb.at[B, rows_of(y2)], left),
        y_copy(2, hb.at[B, rows_of(yr)], right),
        y_copy(3, hb.at[A, rows_of(yl)], left),
        y_copy(4, st.at[0], right),
        y_copy(5, st.at[1], left),
    ]
    for i in range(4):
        ys[i].start()

    loads[4].wait()
    loads[5].wait()
    for i in range(16):
        xf[4 * i : 4 * i + 4, :] = xin[i].astype(F32)
    xin_b = xf[...].astype(BF16)

    def slope(i, carry):
        cols = pl.ds(pl.multiple_of(i * 512, 512), 512)
        hid = jnp.dot(xin_b, win[:, cols], preferred_element_type=F32)
        gp[:, cols] = gelu_slope(hid)
        return carry

    lax.fori_loop(0, 6, slope, 0)

    ys[0].wait_recv()
    st[0] = (ry[0].astype(F32) + hb[A, rows_of(yr), :].astype(F32)).astype(BF16)
    ys[4].start()
    ys[1].wait_recv()
    st[1] = (ry[1].astype(F32) + hb[B, rows_of(yl), :].astype(F32)).astype(BF16)
    ys[5].start()

    def gather(buf, ss, rs):
        return [
            remote(buf.at[y, :, h], buf.at[y, :, h], ss.at[1], rs.at[1], right),
            remote(buf.at[y, :, h], buf.at[y, :, h], ss.at[2], rs.at[2], left),
            remote(buf.at[yl, 0, h], buf.at[yl, 0, h], ss.at[3], rs.at[3], right),
            remote(buf.at[yr, 1, h], buf.at[yr, 1, h], ss.at[4], rs.at[4], left),
            remote(buf.at[:, :, h], buf.at[:, :, h], ss.at[5], rs.at[5], mate),
        ]

    o_g = gather(ob, o_s, o_r)
    p_g = gather(ptb, p_s, p_r)
    z_o.wait_recv()
    o_g[0].start()
    o_g[1].start()

    def colmax(i, m):
        rows = pl.ds(pl.multiple_of(i * 64, 64), 64)
        return jnp.maximum(m, jnp.max(lg[rows, :].astype(F32), axis=0, keepdims=True))

    m_loc = lax.fori_loop(1, 8, colmax, jnp.max(lg[0:64, :].astype(F32), axis=0, keepdims=True))

    def colsum(i, t):
        rows = pl.ds(pl.multiple_of(i * 64, 64), 64)
        return t + jnp.sum(jnp.exp(lg[rows, :].astype(F32) - m_loc), axis=0, keepdims=True)

    s_loc = lax.fori_loop(0, 8, colsum, jnp.zeros((1, 1024), F32))
    stl[0:1, :] = m_loc
    stl[1:2, :] = s_loc

    def st_copy(i):
        return remote(stl, stb.at[s], st_s.at[0], st_r.at[0], group(i))

    own_st = pltpu.make_async_copy(stl, stb.at[s], st_r.at[0])
    own_st.start()

    def st_start(i, carry):
        st_copy(i).start()
        return carry

    lax.fori_loop(1, 16, st_start, 0)

    ys[3].wait_recv()
    ys[4].wait_recv()
    qf[0:8] = hb[A, rows_of(y), :].astype(F32) + ry[3].astype(F32) + ry[4].astype(F32)
    ys[2].wait_recv()
    ys[5].wait_recv()
    qf[8:16] = hb[B, rows_of(y), :].astype(F32) + ry[2].astype(F32) + ry[5].astype(F32)
    for i in range(4):
        a2s[:, i] = qf[:, 4 * i : 4 * i + 4, :].astype(BF16)

    def a_start(i, carry):
        cd, sd = plane(i)
        remote(a2s.at[cd, sd % 4], a2r.at[c * 4 + q], a_s.at[0], a_r.at[0], (cd, sd)).start()
        return carry

    pltpu.make_async_copy(a2s.at[c, q], a2r.at[c * 4 + q], a_r.at[0]).start()
    lax.fori_loop(1, 64, a_start, 0)

    z_p.wait_recv()
    p_g[0].start()
    p_g[1].start()
    o_g[0].wait_recv()
    o_g[2].start()
    o_g[1].wait_recv()
    o_g[3].start()

    pltpu.make_async_copy(stb, stb, st_r.at[0]).wait()
    m_all = stb[:, 0, :]
    top = jnp.max(m_all, axis=0, keepdims=True)
    total = jnp.sum(stb[:, 1, :] * jnp.exp(m_all - top), axis=0, keepdims=True)
    inv_total = 1.0 / total

    def disp(i, carry):
        rows = pl.ds(pl.multiple_of(i * 64, 64), 64)
        d = jnp.exp(lg[rows, :].astype(F32) - top) * inv_total
        dspf[rows, :] = d
        dspb[rows, :] = d.astype(BF16)
        return carry

    lax.fori_loop(0, 8, disp, 0)

    loads[6].wait()
    pltpu.make_async_copy(a2r, a2r, a_r.at[0]).wait()
    for i in range(16):
        for j in range(2):
            xf[4 * i : 4 * i + 4, 384 * j : 384 * j + 384] = (
                a2r[4 * i + j].astype(F32) + a2r[4 * i + 2 + j].astype(F32)
            )
    x_b = xf[...].astype(BF16)
    xf[...] = jnp.zeros((64, 768), F32)

    def expert(i, carry):
        part = pl.ds(pl.multiple_of(i * 512, 512), 512)
        act = lax.dot_general(x_b, wout[part, :], NT, preferred_element_type=F32)
        hc = (act * gp[:, part]).astype(BF16)
        xf[...] += lax.dot_general(hc, win[:, part], NT, preferred_element_type=F32)
        return carry

    lax.fori_loop(0, 6, expert, 0)
    for i in range(16):
        for j in range(2):
            b2s[i, j] = xf[4 * i : 4 * i + 4, 384 * j : 384 * j + 384].astype(BF16)

    def b_start(i, carry):
        cd, sd = plane(i)
        remote(b2s.at[cd, sd % 2], b2r.at[c * 4 + q], b_s.at[0], b_r.at[0], (cd, sd)).start()
        return carry

    pltpu.make_async_copy(b2s.at[c, h], b2r.at[c * 4 + q], b_r.at[0]).start()
    lax.fori_loop(1, 64, b_start, 0)

    o_g[2].wait_recv()
    o_g[3].wait_recv()
    o_g[4].start()
    p_g[0].wait_recv()
    p_g[2].start()
    p_g[1].wait_recv()
    p_g[3].start()
    o_g[4].wait_recv()

    def comb_dot(i, carry):
        cols = pl.ds(pl.multiple_of(i * 256, 256), 256)
        w = ob[i].reshape(256, 768)
        cc[:, cols] = lax.dot_general(og[...], w, NT, preferred_element_type=F32)
        return carry

    lax.fori_loop(0, 4, comb_dot, 0)

    def comb_grad(i, carry):
        rows = pl.ds(pl.multiple_of(i * 64, 64), 64)
        comb = cf[rows, :]
        v = cc[rows, :]
        cc[rows, :] = comb * (v - jnp.sum(comb * v, axis=1, keepdims=True))
        return carry

    lax.fori_loop(0, 8, comb_grad, 0)
    p_g[2].wait_recv()
    p_g[3].wait_recv()
    p_g[4].start()

    loads[7].wait()
    pltpu.make_async_copy(b2r, b2r, b_r.at[0]).wait()
    back = b2r[...].reshape(16, 4, 4, 384)
    for i in range(4):
        zf[:, 4 * i : 4 * i + 4, :] = back[:, i].astype(F32)
    sgb[:, rows_of(y), mine] = zf[...].astype(BF16)

    def g_copy(i, part, yy, dev):
        ref = sgb.at[part, rows_of(yy), mine]
        return remote(ref, ref, g_s.at[i], g_r.at[i], dev)

    def k_copy(i, part, yy):
        ref = sgb.at[part, rows_of(yy), mine]
        return remote(ref, ref, k_s.at[i], k_r.at[i], mate)

    gs = [
        g_copy(0, A, y, right),
        g_copy(1, B, y, left),
        g_copy(2, B, y, right),
        g_copy(3, A, y, left),
        g_copy(4, A, yl, right),
        g_copy(5, B, yr, left),
    ]
    ks = [
        k_copy(0, A, y),
        k_copy(1, B, y),
        k_copy(2, A, yl),
        k_copy(3, B, yr),
        k_copy(4, B, yl),
        k_copy(5, A, yr),
        k_copy(6, A, y2),
        k_copy(7, B, y2),
    ]
    for i in range(4):
        gs[i].start()
    ks[0].start()
    ks[1].start()
    gs[0].wait_recv()
    gs[4].start()
    ks[2].start()
    gs[1].wait_recv()
    gs[5].start()
    ks[3].start()
    for i in range(2, 6):
        gs[i].wait_recv()
        ks[i + 2].start()
    for k in ks:
        k.wait_recv()

    def disp_dot(i, carry):
        cols = pl.ds(pl.multiple_of(i * 256, 256), 256)
        w = sgb[pl.ds(i * 4, 4)].reshape(256, 768)
        d = lax.dot_general(tok[...], w, NT, preferred_element_type=F32) * dspf[:, cols]
        ddf[:, cols] = d
        dtl[:, cols] = jnp.sum(d, axis=0, keepdims=True)
        return carry

    lax.fori_loop(0, 4, disp_dot, 0)

    def dt_copy(i):
        return remote(dtl, dtb.at[s], dt_s.at[0], dt_r.at[0], group(i))

    pltpu.make_async_copy(dtl, dtb.at[s], dt_r.at[0]).start()

    def dt_start(i, carry):
        dt_copy(i).start()
        return carry

    lax.fori_loop(1, 16, dt_start, 0)

    def direct(i, carry):
        cols = pl.ds(pl.multiple_of(i * 256, 256), 256)
        w = sgb[:, :, cols].reshape(1024, 256)
        acc[:, cols] = jnp.dot(dspb[...], w, preferred_element_type=F32)
        return carry

    lax.fori_loop(0, 3, direct, 0)
    p_g[4].wait_recv()
    pltpu.make_async_copy(dtb, dtb, dt_r.at[0]).wait()
    dots = jnp.sum(dtb[...], axis=0)

    def logit(i, carry):
        rows = pl.ds(pl.multiple_of(i * 64, 64), 64)
        cb[rows, :] = (cc[rows, :] + ddf[rows, :] - dspf[rows, :] * dots).astype(BF16)
        return carry

    lax.fori_loop(0, 8, logit, 0)

    def through(i, carry):
        cols = pl.ds(pl.multiple_of(i * 256, 256), 256)
        w = ptb[:, :, :, :, cols].reshape(1024, 256)
        t = acc[:, cols] + jnp.dot(cb[...], w, preferred_element_type=F32)
        out_ref[0, :, cols] = t.astype(BF16)
        return carry

    lax.fori_loop(0, 3, through, 0)

    for k in range(4):
        cs_copy(k).wait_send()
    for copy in ys + gs + ks + o_g + p_g + [z_o, z_p]:
        copy.wait_send()

    def drain(buf_src, sem):
        pltpu.make_async_copy(buf_src, buf_src, sem).wait()

    drain(a2r.at[pl.ds(0, 63)], a_s.at[0])
    drain(b2r.at[pl.ds(0, 63)], b_s.at[0])
    drain(stb.at[pl.ds(0, 15)], st_s.at[0])
    drain(dtb.at[pl.ds(0, 15)], dt_s.at[0])


def on_device(tokens, out_grad, saved_logits, slot_params, slot_inputs, slot_outputs, expert_in, expert_out):
    any_spec = pl.BlockSpec(memory_space=pl.ANY)
    vm = pltpu.VMEM
    dma = pltpu.SemaphoreType.DMA
    return pl.pallas_call(
        kernel,
        out_shape=jax.ShapeDtypeStruct((1, 512, 768), BF16),
        in_specs=[any_spec] * 8,
        out_specs=pl.BlockSpec(memory_space=pltpu.VMEM),
        scratch_shapes=[
            vm((512, 1024), BF16),
            vm((512, 768), BF16),
            vm((512, 768), BF16),
            vm((768, 3072), BF16),
            vm((3072, 768), BF16),
            vm((16, 4, 768), BF16),
            vm((512, 1024), F32),
            vm((512, 1024), BF16),
            vm((16, 64, 768), BF16),
            vm((16, 64, 384), BF16),
            vm((16, 64, 384), BF16),
            vm((6, 8, 16, 384), BF16),
            vm((2, 8, 16, 384), BF16),
            vm((16, 16, 384), F32),
            vm((16, 4, 4, 384), BF16),
            vm((64, 4, 384), BF16),
            vm((64, 768), F32),
            vm((64, 3072), F32),
            vm((16, 2, 4, 384), BF16),
            vm((64, 4, 384), BF16),
            vm((16, 16, 384), F32),
            vm((16, 64, 768), BF16),
            vm((4, 2, 2, 64, 768), BF16),
            vm((4, 2, 2, 64, 768), BF16),
            vm((512, 1024), F32),
            vm((512, 1024), F32),
            vm((512, 1024), F32),
            vm((512, 1024), BF16),
            vm((2, 1024), F32),
            vm((16, 2, 1024), F32),
            vm((1, 1024), F32),
            vm((16, 1, 1024), F32),
            vm((512, 768), F32),
            dma((8,)),
            dma((4,)), dma((4,)),
            dma((6,)), dma((6,)),
            dma((1,)), dma((1,)),
            dma((1,)), dma((1,)),
            dma((6,)), dma((6,)),
            dma((8,)), dma((8,)),
            dma((6,)), dma((6,)),
            dma((6,)), dma((6,)),
            dma((1,)), dma((1,)),
            dma((1,)), dma((1,)),
        ],
        compiler_params=pltpu.CompilerParams(
            collective_id=0, has_side_effects=True, vmem_limit_bytes=60 * 1024 * 1024
        ),
    )(tokens, out_grad, saved_logits, slot_params.T, slot_inputs, slot_outputs, expert_in, expert_out)


def solution(mesh):
    placed = (
        P("clip", "seq", None),
        P("clip", "seq", None),
        P("clip", "seq", None),
        P(None, "seq"),
        P(None, ("clip", "seq"), None),
        P("clip", "seq", None),
        P(("clip", "seq"), None, None),
        P(("clip", "seq"), None, None),
    )
    return jax.shard_map(
        on_device, mesh=mesh, in_specs=placed, out_specs=P("clip", "seq", None), check_vma=False
    )
```

```python
import jax
import jax.numpy as jnp
from jax import lax
from jax.experimental import pallas as pl
from jax.experimental.pallas import tpu as pltpu
from jax.sharding import PartitionSpec as P

F32 = jnp.float32
BF16 = jnp.bfloat16
MESH = pl.DeviceIdType.MESH
NT = (((1,), (1,)), ((), ()))
TN = (((0,), (0,)), ((), ()))


def gelu_slope(x):
    k = 0.7978845608028654
    t = jnp.tanh(k * (x + 0.044715 * x * x * x))
    return 0.5 * (1.0 + t) + 0.5 * x * (1.0 - t * t) * (k * (1.0 + 0.134145 * x * x))


def kernel(
    tok_h, og_h, lg_h, pt_h, xin_h, so_h, win_h, wout_h, out_ref,
    lg, og, tok, win, wout, xin, cf, cb, pb, rp, hb, ry, st, qf, a2s, a2r, xf, gp, hc, b2s, b2r, zf, sgb,
    ob, ptb, cc, ddf, dspf, dspb, stl, stb, dtl, dtb, acc,
    ld, cs_s, cs_r, y_s, y_r, a_s, a_r, b_s, b_r, g_s, g_r, k_s, k_r, o_s, o_r, p_s, p_r, st_s, st_r, dt_s, dt_r,
):
    c = lax.axis_index("clip")
    s = lax.axis_index("seq")
    y, q, h = s // 4, s % 4, s % 2
    zl = q // 2
    yr, y2, yl = (y + 1) % 4, (y + 2) % 4, (y + 3) % 4
    right, left = (c, yr * 4 + q), (c, yl * 4 + q)
    mate = (c, s + 1 - 2 * h)
    zmate = (c, s + 2 - 4 * zl)
    mine = pl.ds(pl.multiple_of(h * 384, 128), 384)
    other = pl.ds(pl.multiple_of((1 - h) * 384, 128), 384)

    def rows_of(yy):
        return pl.ds(pl.multiple_of(yy * 16, 16), 16)

    def remote(src, dst, ssem, rsem, dev):
        return pltpu.make_async_remote_copy(
            src_ref=src, dst_ref=dst, send_sem=ssem, recv_sem=rsem, device_id=dev, device_id_type=MESH
        )

    def far(k):
        return ((c // 4 + 3 - k // 4) % 4) * 4 + (c + 3 - k % 4) % 4

    def to_plane(send):
        def step(k, carry):
            for t in range(4):
                send(far(k), t)
            return carry

        lax.fori_loop(0, 15, step, 0)
        for t in range(1, 4):
            send(c, (q + t) % 4)

    def group(i):
        return (c, (s + i) % 16)

    loads = [
        pltpu.make_async_copy(lg_h.at[0], lg, ld.at[0]),
        pltpu.make_async_copy(og_h.at[0], og, ld.at[1]),
        pltpu.make_async_copy(so_h.at[0], ob.at[y, zl, h], ld.at[2]),
        pltpu.make_async_copy(pt_h, ptb.at[y, zl, h], ld.at[3]),
        pltpu.make_async_copy(xin_h, xin, ld.at[4]),
        pltpu.make_async_copy(win_h.at[0], win, ld.at[5]),
        pltpu.make_async_copy(wout_h.at[0], wout, ld.at[6]),
        pltpu.make_async_copy(tok_h.at[0], tok, ld.at[7]),
    ]
    for load in loads:
        load.start()

    barrier = pltpu.get_barrier_semaphore()

    def greet_plane(cd, t):
        pl.semaphore_signal(barrier, inc=1, device_id=(cd, y * 4 + t), device_id_type=MESH)

    def greet_group(i, carry):
        pl.semaphore_signal(
            barrier, inc=1, device_id=(c, ((y + 1 + i // 4) % 4) * 4 + i % 4), device_id_type=MESH
        )
        return carry

    to_plane(greet_plane)
    lax.fori_loop(0, 12, greet_group, 0)

    loads[0].wait()

    def front(i, carry):
        rows = pl.ds(pl.multiple_of(i * 64, 64), 64)
        l = lg[rows, :].astype(F32)
        e = jnp.exp(l - jnp.max(l, axis=1, keepdims=True))
        comb = e * (1.0 / jnp.sum(e, axis=1, keepdims=True))
        cf[rows, :] = comb
        cb[rows, :] = comb.astype(BF16)
        return carry

    lax.fori_loop(0, 8, front, 0, unroll=2)
    loads[1].wait()

    def cs_copy(k):
        part = pl.ds(k * 4, 4)
        return remote(pb.at[part, :, other], rp.at[part], cs_s.at[k], cs_r.at[k], mate)

    def partial(k, carry):
        cols = pl.ds(pl.multiple_of(k * 256, 256), 256)
        p = lax.dot_general(cb[:, cols], og[...], TN, preferred_element_type=F32)
        pb[pl.ds(k * 4, 4)] = p.astype(BF16).reshape(4, 64, 768)
        return carry

    lax.fori_loop(0, 3, partial, 0)
    pl.semaphore_wait(barrier, 75)
    for k in range(3):
        cs_copy(k).start()
    partial(3, 0)
    cs_copy(3).start()

    loads[2].wait()
    loads[3].wait()
    z_o = remote(ob.at[y, zl, h], ob.at[y, zl, h], o_s.at[0], o_r.at[0], zmate)
    z_p = remote(ptb.at[y, zl, h], ptb.at[y, zl, h], p_s.at[0], p_r.at[0], zmate)
    z_o.start()
    z_p.start()

    def half_sum(k, carry):
        part = pl.ds(k * 4, 4)
        cs_copy(k).wait_recv()
        hb[part] = (pb[part, :, mine].astype(F32) + rp[part].astype(F32)).astype(BF16)
        return carry

    lax.fori_loop(0, 4, half_sum, 0)

    A, B = pl.ds(0, 8), pl.ds(8, 8)

    def y_copy(i, src, dev):
        return remote(src, ry.at[i], y_s.at[i], y_r.at[i], dev)

    ys = [
        y_copy(0, hb.at[A, rows_of(y2)], right),
        y_copy(1, hb.at[B, rows_of(y2)], left),
        y_copy(2, hb.at[B, rows_of(yr)], right),
        y_copy(3, hb.at[A, rows_of(yl)], left),
        y_copy(4, st.at[0], right),
        y_copy(5, st.at[1], left),
    ]
    ys[0].start()
    ys[1].start()

    loads[4].wait()
    loads[5].wait()
    for i in range(16):
        xf[4 * i : 4 * i + 4, :] = xin[i].astype(F32)
    xin_b = xf[...].astype(BF16)

    def slope(i, carry):
        part = pl.ds(pl.multiple_of(i * 512, 512), 512)
        hid = jnp.dot(xin_b, win[:, part], preferred_element_type=F32)
        gp[:, part] = gelu_slope(hid)
        return carry

    lax.fori_loop(0, 3, slope, 0)
    ys[0].wait_send()
    ys[1].wait_send()
    ys[2].start()
    ys[3].start()
    lax.fori_loop(3, 6, slope, 0)

    ys[0].wait_recv()
    st[0] = (ry[0].astype(F32) + hb[A, rows_of(yr), :].astype(F32)).astype(BF16)
    ys[4].start()
    ys[1].wait_recv()
    st[1] = (ry[1].astype(F32) + hb[B, rows_of(yl), :].astype(F32)).astype(BF16)
    ys[5].start()

    def gather(buf, ss, rs):
        return [
            remote(buf.at[y, :, h], buf.at[y, :, h], ss.at[1], rs.at[1], right),
            remote(buf.at[y, :, h], buf.at[y, :, h], ss.at[2], rs.at[2], left),
            remote(buf.at[yl, 0, h], buf.at[yl, 0, h], ss.at[3], rs.at[3], right),
            remote(buf.at[yr, 1, h], buf.at[yr, 1, h], ss.at[4], rs.at[4], left),
            remote(buf.at[:, :, h], buf.at[:, :, h], ss.at[5], rs.at[5], mate),
        ]

    o_g = gather(ob, o_s, o_r)
    p_g = gather(ptb, p_s, p_r)
    def colmax(i, m):
        rows = pl.ds(pl.multiple_of(i * 64, 64), 64)
        return jnp.maximum(m, jnp.max(lg[rows, :].astype(F32), axis=0, keepdims=True))

    m_loc = lax.fori_loop(1, 8, colmax, jnp.max(lg[0:64, :].astype(F32), axis=0, keepdims=True))

    def colsum(i, t):
        rows = pl.ds(pl.multiple_of(i * 64, 64), 64)
        return t + jnp.sum(jnp.exp(lg[rows, :].astype(F32) - m_loc), axis=0, keepdims=True)

    s_loc = lax.fori_loop(0, 8, colsum, jnp.zeros((1, 1024), F32))
    stl[0:1, :] = m_loc
    stl[1:2, :] = s_loc

    def st_copy(i):
        return remote(stl, stb.at[s], st_s.at[0], st_r.at[0], group(i))

    own_st = pltpu.make_async_copy(stl, stb.at[s], st_r.at[0])
    own_st.start()

    def st_start(i, carry):
        st_copy(i).start()
        return carry

    lax.fori_loop(1, 16, st_start, 0)

    ys[4].wait_send()
    ys[5].wait_send()
    z_o.wait_recv()
    o_g[0].start()
    o_g[1].start()
    ys[3].wait_recv()
    ys[4].wait_recv()
    qf[0:8] = hb[A, rows_of(y), :].astype(F32) + ry[3].astype(F32) + ry[4].astype(F32)
    ys[2].wait_recv()
    ys[5].wait_recv()
    qf[8:16] = hb[B, rows_of(y), :].astype(F32) + ry[2].astype(F32) + ry[5].astype(F32)
    for i in range(4):
        a2s[:, i] = qf[:, 4 * i : 4 * i + 4, :].astype(BF16)

    def a_start(cd, t):
        remote(a2s.at[cd, t], a2r.at[c * 4 + q], a_s.at[0], a_r.at[0], (cd, y * 4 + t)).start()

    pltpu.make_async_copy(a2s.at[c, q], a2r.at[c * 4 + q], a_r.at[0]).start()
    to_plane(a_start)

    z_p.wait_recv()
    p_g[0].start()
    p_g[1].start()
    o_g[0].wait_recv()
    o_g[2].start()
    o_g[1].wait_recv()
    o_g[3].start()

    pltpu.make_async_copy(stb, stb, st_r.at[0]).wait()
    m_all = stb[:, 0, :]
    top = jnp.max(m_all, axis=0, keepdims=True)
    total = jnp.sum(stb[:, 1, :] * jnp.exp(m_all - top), axis=0, keepdims=True)
    inv_total = 1.0 / total

    def disp(i, carry):
        rows = pl.ds(pl.multiple_of(i * 64, 64), 64)
        d = jnp.exp(lg[rows, :].astype(F32) - top) * inv_total
        dspf[rows, :] = d
        dspb[rows, :] = d.astype(BF16)
        return carry

    lax.fori_loop(0, 8, disp, 0)

    loads[6].wait()
    pltpu.make_async_copy(a2r, a2r, a_r.at[0]).wait()
    for i in range(16):
        for j in range(2):
            xf[4 * i : 4 * i + 4, 384 * j : 384 * j + 384] = (
                a2r[4 * i + j].astype(F32) + a2r[4 * i + 2 + j].astype(F32)
            )
    x_b = xf[...].astype(BF16)

    def act(i, carry):
        part = pl.ds(pl.multiple_of(i * 1024, 1024), 1024)
        a = lax.dot_general(x_b, wout[part, :], NT, preferred_element_type=F32)
        hc[:, part] = (a * gp[:, part]).astype(BF16)
        return carry

    lax.fori_loop(0, 3, act, 0)

    def grad(i, carry):
        part = pl.ds(pl.multiple_of(i * 256, 256), 256)
        xf[:, part] = lax.dot_general(hc[...], win[part, :], NT, preferred_element_type=F32)
        return carry

    lax.fori_loop(0, 3, grad, 0)
    for i in range(16):
        for j in range(2):
            b2s[i, j] = xf[4 * i : 4 * i + 4, 384 * j : 384 * j + 384].astype(BF16)

    def b_start(cd, t):
        remote(b2s.at[cd, t % 2], b2r.at[c * 4 + q], b_s.at[0], b_r.at[0], (cd, y * 4 + t)).start()

    pltpu.make_async_copy(b2s.at[c, h], b2r.at[c * 4 + q], b_r.at[0]).start()
    to_plane(b_start)

    o_g[2].wait_recv()
    o_g[3].wait_recv()
    o_g[4].start()
    p_g[0].wait_recv()
    p_g[2].start()
    p_g[1].wait_recv()
    p_g[3].start()
    o_g[4].wait_recv()

    def comb_dot(i, carry):
        cols = pl.ds(pl.multiple_of(i * 256, 256), 256)
        w = ob[i].reshape(256, 768)
        cc[:, cols] = lax.dot_general(og[...], w, NT, preferred_element_type=F32)
        return carry

    lax.fori_loop(0, 4, comb_dot, 0)

    def comb_grad(i, carry):
        rows = pl.ds(pl.multiple_of(i * 64, 64), 64)
        comb = cf[rows, :]
        v = cc[rows, :]
        cc[rows, :] = comb * (v - jnp.sum(comb * v, axis=1, keepdims=True))
        return carry

    lax.fori_loop(0, 8, comb_grad, 0)
    p_g[2].wait_recv()
    p_g[3].wait_recv()
    p_g[4].start()

    loads[7].wait()
    pltpu.make_async_copy(b2r, b2r, b_r.at[0]).wait()
    back = b2r[...].reshape(16, 4, 4, 384)
    for i in range(4):
        zf[:, 4 * i : 4 * i + 4, :] = back[:, i].astype(F32)
    sgb[:, rows_of(y), mine] = zf[...].astype(BF16)

    def g_copy(i, part, yy, dev):
        ref = sgb.at[part, rows_of(yy), mine]
        return remote(ref, ref, g_s.at[i], g_r.at[i], dev)

    def k_copy(i, part, yy):
        ref = sgb.at[part, rows_of(yy), mine]
        return remote(ref, ref, k_s.at[i], k_r.at[i], mate)

    gs = [
        g_copy(0, A, y, right),
        g_copy(1, B, y, left),
        g_copy(2, B, y, right),
        g_copy(3, A, y, left),
        g_copy(4, A, yl, right),
        g_copy(5, B, yr, left),
    ]
    ks = [
        k_copy(0, A, y),
        k_copy(1, B, y),
        k_copy(2, A, yl),
        k_copy(3, B, yr),
        k_copy(4, B, yl),
        k_copy(5, A, yr),
        k_copy(6, A, y2),
        k_copy(7, B, y2),
    ]
    gs[0].start()
    gs[1].start()
    ks[0].start()
    ks[1].start()
    gs[0].wait_send()
    gs[1].wait_send()
    gs[2].start()
    gs[3].start()
    gs[0].wait_recv()
    gs[4].start()
    ks[2].start()
    gs[1].wait_recv()
    gs[5].start()
    ks[3].start()
    for i in range(2, 6):
        gs[i].wait_recv()
        ks[i + 2].start()
    for k in ks:
        k.wait_recv()

    def disp_dot(i, carry):
        cols = pl.ds(pl.multiple_of(i * 256, 256), 256)
        w = sgb[pl.ds(i * 4, 4)].reshape(256, 768)
        d = lax.dot_general(tok[...], w, NT, preferred_element_type=F32) * dspf[:, cols]
        ddf[:, cols] = d
        dtl[:, cols] = jnp.sum(d, axis=0, keepdims=True)
        return carry

    lax.fori_loop(0, 4, disp_dot, 0)

    def dt_copy(i):
        return remote(dtl, dtb.at[s], dt_s.at[0], dt_r.at[0], group(i))

    pltpu.make_async_copy(dtl, dtb.at[s], dt_r.at[0]).start()

    def dt_start(i, carry):
        dt_copy(i).start()
        return carry

    lax.fori_loop(1, 16, dt_start, 0)

    def direct(i, carry):
        cols = pl.ds(pl.multiple_of(i * 256, 256), 256)
        w = sgb[:, :, cols].reshape(1024, 256)
        acc[:, cols] = jnp.dot(dspb[...], w, preferred_element_type=F32)
        return carry

    lax.fori_loop(0, 3, direct, 0)
    p_g[4].wait_recv()
    pltpu.make_async_copy(dtb, dtb, dt_r.at[0]).wait()
    dots = jnp.sum(dtb[...], axis=0)

    def logit(i, carry):
        rows = pl.ds(pl.multiple_of(i * 64, 64), 64)
        cb[rows, :] = (cc[rows, :] + ddf[rows, :] - dspf[rows, :] * dots).astype(BF16)
        return carry

    lax.fori_loop(0, 8, logit, 0)

    def through(i, carry):
        cols = pl.ds(pl.multiple_of(i * 256, 256), 256)
        w = ptb[:, :, :, :, cols].reshape(1024, 256)
        t = acc[:, cols] + jnp.dot(cb[...], w, preferred_element_type=F32)
        out_ref[0, :, cols] = t.astype(BF16)
        return carry

    lax.fori_loop(0, 3, through, 0)

    for k in range(4):
        cs_copy(k).wait_send()
    for copy in ys[2:4] + gs[2:] + ks + o_g + p_g + [z_o, z_p]:
        copy.wait_send()

    def drain(buf_src, sem):
        pltpu.make_async_copy(buf_src, buf_src, sem).wait()

    drain(a2r.at[pl.ds(0, 63)], a_s.at[0])
    drain(b2r.at[pl.ds(0, 63)], b_s.at[0])
    drain(stb.at[pl.ds(0, 15)], st_s.at[0])
    drain(dtb.at[pl.ds(0, 15)], dt_s.at[0])


def on_device(tokens, out_grad, saved_logits, slot_params, slot_inputs, slot_outputs, expert_in, expert_out):
    any_spec = pl.BlockSpec(memory_space=pl.ANY)
    vm = pltpu.VMEM
    dma = pltpu.SemaphoreType.DMA
    return pl.pallas_call(
        kernel,
        out_shape=pltpu.VMEM((1, 512, 768), BF16),
        in_specs=[any_spec] * 8,
        out_specs=pl.BlockSpec(memory_space=pltpu.VMEM),
        scratch_shapes=[
            vm((512, 1024), BF16),
            vm((512, 768), BF16),
            vm((512, 768), BF16),
            vm((768, 3072), BF16),
            vm((3072, 768), BF16),
            vm((16, 4, 768), BF16),
            vm((512, 1024), F32),
            vm((512, 1024), BF16),
            vm((16, 64, 768), BF16),
            vm((16, 64, 384), BF16),
            vm((16, 64, 384), BF16),
            vm((6, 8, 16, 384), BF16),
            vm((2, 8, 16, 384), BF16),
            vm((16, 16, 384), F32),
            vm((16, 4, 4, 384), BF16),
            vm((64, 4, 384), BF16),
            vm((64, 768), F32),
            vm((64, 3072), F32),
            vm((64, 3072), BF16),
            vm((16, 2, 4, 384), BF16),
            vm((64, 4, 384), BF16),
            vm((16, 16, 384), F32),
            vm((16, 64, 768), BF16),
            vm((4, 2, 2, 64, 768), BF16),
            vm((4, 2, 2, 64, 768), BF16),
            vm((512, 1024), F32),
            vm((512, 1024), F32),
            vm((512, 1024), F32),
            vm((512, 1024), BF16),
            vm((2, 1024), F32),
            vm((16, 2, 1024), F32),
            vm((1, 1024), F32),
            vm((16, 1, 1024), F32),
            vm((512, 768), F32),
            dma((8,)),
            dma((4,)), dma((4,)),
            dma((6,)), dma((6,)),
            dma((1,)), dma((1,)),
            dma((1,)), dma((1,)),
            dma((6,)), dma((6,)),
            dma((8,)), dma((8,)),
            dma((6,)), dma((6,)),
            dma((6,)), dma((6,)),
            dma((1,)), dma((1,)),
            dma((1,)), dma((1,)),
        ],
        compiler_params=pltpu.CompilerParams(
            collective_id=0, has_side_effects=True, vmem_limit_bytes=60 * 1024 * 1024
        ),
    )(tokens, out_grad, saved_logits, slot_params.T, slot_inputs, slot_outputs, expert_in, expert_out)


def solution(mesh):
    placed = (
        P("clip", "seq", None),
        P("clip", "seq", None),
        P("clip", "seq", None),
        P(None, "seq"),
        P(None, ("clip", "seq"), None),
        P("clip", "seq", None),
        P(("clip", "seq"), None, None),
        P(("clip", "seq"), None, None),
    )
    return jax.shard_map(
        on_device, mesh=mesh, in_specs=placed, out_specs=P("clip", "seq", None), check_vma=False
    )
```

```python
import jax
import jax.numpy as jnp
from jax import lax
from jax.experimental import pallas as pl
from jax.experimental.pallas import tpu as pltpu
from jax.sharding import PartitionSpec as P

F32 = jnp.float32
BF16 = jnp.bfloat16
MESH = pl.DeviceIdType.MESH
NT = (((1,), (1,)), ((), ()))
TN = (((0,), (0,)), ((), ()))


def gelu_slope(x):
    k = 0.7978845608028654
    t = jnp.tanh(k * (x + 0.044715 * x * x * x))
    return 0.5 * (1.0 + t) + 0.5 * x * (1.0 - t * t) * (k * (1.0 + 0.134145 * x * x))


def kernel(
    tok_h, og_h, lg_h, pt_h, xin_h, so_h, win_h, wout_h, out_ref,
    lg, og, tok, win, wout, xin, cf, cb, pb, rp, hb, ry, st, qf, a2s, a2r, xf, gp, hc, b2s, b2r, zf, sp,
    ob, cc, dspf, lw, stl, s1b, s1l, s2b, dtl, dtb, acc, lgp, xp, xrp, hx, xry, xst, xq,
    ld, cs_s, cs_r, y_s, y_r, a_s, a_r, b_s, b_r, g_s, g_r, k_s, k_r, o_s, o_r, p_s, p_r, s1_s, s1_r, s2_s, s2_r, dt_s, dt_r, xc_s, xc_r, x_s, x_r,
):
    sgb, ptx = sp.at[0], sp.at[1].reshape(4, 2, 2, 4, 16, 768)
    c = lax.axis_index("clip")
    s = lax.axis_index("seq")
    y, q, h = s // 4, s % 4, s % 2
    zl = q // 2
    x, zh = c // 4, c % 4
    xr, xl = (x + 1) % 4, (x + 3) % 4
    yr, y2, yl = (y + 1) % 4, (y + 2) % 4, (y + 3) % 4
    right, left = (c, yr * 4 + q), (c, yl * 4 + q)
    mate = (c, s + 1 - 2 * h)
    zmate = (c, s + 2 - 4 * zl)
    mine = pl.ds(pl.multiple_of(h * 384, 128), 384)
    other = pl.ds(pl.multiple_of((1 - h) * 384, 128), 384)

    def rows_of(yy):
        return pl.ds(pl.multiple_of(yy * 16, 16), 16)

    def remote(src, dst, ssem, rsem, dev):
        return pltpu.make_async_remote_copy(
            src_ref=src, dst_ref=dst, send_sem=ssem, recv_sem=rsem, device_id=dev, device_id_type=MESH
        )

    def far(k):
        return ((c // 4 + 3 - k // 4) % 4) * 4 + (c + 3 - k % 4) % 4

    def to_plane(send):
        def step(k, carry):
            for t in range(4):
                send(far(k), t)
            return carry

        lax.fori_loop(0, 15, step, 0)
        for t in range(1, 4):
            send(c, (q + t) % 4)

    def group(i):
        return (c, (s + i) % 16)

    loads = [
        pltpu.make_async_copy(lg_h.at[0], lg, ld.at[0]),
        pltpu.make_async_copy(og_h.at[0], og, ld.at[1]),
        pltpu.make_async_copy(so_h.at[0], ob.at[y, zl, h], ld.at[2]),
        pltpu.make_async_copy(pt_h.at[rows_of(x)], ptx.at[y, zl, h, x], ld.at[3]),
        pltpu.make_async_copy(xin_h, xin, ld.at[4]),
        pltpu.make_async_copy(win_h.at[0], win, ld.at[5]),
        pltpu.make_async_copy(wout_h.at[0], wout, ld.at[6]),
        pltpu.make_async_copy(tok_h.at[0], tok, ld.at[7]),
    ]
    for load in loads:
        load.start()

    barrier = pltpu.get_barrier_semaphore()

    def greet_plane(cd, t):
        pl.semaphore_signal(barrier, inc=1, device_id=(cd, y * 4 + t), device_id_type=MESH)

    def greet_group(i, carry):
        pl.semaphore_signal(
            barrier, inc=1, device_id=(c, ((y + 1 + i // 4) % 4) * 4 + i % 4), device_id_type=MESH
        )
        return carry

    to_plane(greet_plane)
    lax.fori_loop(0, 12, greet_group, 0)

    loads[0].wait()

    def front(i, carry):
        rows = pl.ds(pl.multiple_of(i * 64, 64), 64)
        l = lg[rows, :].astype(F32)
        e = jnp.exp(l - jnp.max(l, axis=1, keepdims=True))
        comb = e * (1.0 / jnp.sum(e, axis=1, keepdims=True))
        cf[rows, :] = comb
        cb[rows, :] = comb.astype(BF16)
        return carry

    lax.fori_loop(0, 8, front, 0, unroll=2)
    loads[1].wait()

    def cs_copy(i):
        part = rows_of((y + 2 + i) % 4)
        return remote(pb.at[:, part, other], rp.at[:, part], cs_s.at[0], cs_r.at[i], mate)

    def partial(k, carry):
        cols = pl.ds(pl.multiple_of(k * 256, 256), 256)
        p = lax.dot_general(cb[:, cols], og[...], TN, preferred_element_type=F32)
        pb[pl.ds(k * 4, 4)] = p.astype(BF16).reshape(4, 64, 768)
        return carry

    lax.fori_loop(0, 4, partial, 0)
    pl.semaphore_wait(barrier, 75)
    for i in range(4):
        cs_copy(i).start()

    def p_copy(i, ref, dev):
        return remote(ref, ref, p_s.at[i], p_r.at[i], dev)

    x_right, x_left = (xr * 4 + zh, s), (xl * 4 + zh, s)
    ps = [
        p_copy(0, ptx.at[y, zl, h, x], right),
        p_copy(1, ptx.at[y, zl, h, x], left),
        p_copy(2, ptx.at[y, zl, h, x], (c, y2 * 4 + q)),
        p_copy(3, ptx.at[:, zl, h, x], zmate),
        p_copy(4, ptx.at[:, :, h, x], x_right),
        p_copy(5, ptx.at[:, :, h, x], x_left),
        p_copy(6, ptx.at[:, 0, h, xl], x_right),
        p_copy(7, ptx.at[:, 1, h, xr], x_left),
        p_copy(8, ptx.at[:, :, h], mate),
    ]
    loads[2].wait()
    loads[3].wait()
    z_o = remote(ob.at[y, zl, h], ob.at[y, zl, h], o_s.at[0], o_r.at[0], zmate)
    z_o.start()
    for i in range(3):
        ps[i].start()

    def half_sum(i):
        part = rows_of((y + 2 + i) % 4)
        cs_copy(i).wait_recv()
        hb[:, part, :] = (pb[:, part, mine].astype(F32) + rp[:, part, :].astype(F32)).astype(BF16)

    A, B = pl.ds(0, 8), pl.ds(8, 8)

    def y_copy(i, src, dev):
        return remote(src, ry.at[i], y_s.at[i], y_r.at[i], dev)

    ys = [
        y_copy(0, hb.at[A, rows_of(y2)], right),
        y_copy(1, hb.at[B, rows_of(y2)], left),
        y_copy(2, hb.at[B, rows_of(yr)], right),
        y_copy(3, hb.at[A, rows_of(yl)], left),
        y_copy(4, st.at[0], right),
        y_copy(5, st.at[1], left),
    ]
    half_sum(0)
    ys[0].start()
    ys[1].start()
    for i in range(1, 4):
        half_sum(i)

    def reorder(k, carry):
        p = lax.broadcasted_iota(jnp.int32, (1, 256), 1)
        pick = lax.broadcasted_iota(jnp.int32, (1024, 256), 0) == (p // 16) * 64 + p % 16 + k * 16
        part = jnp.dot(lg[...], pick.astype(F32).astype(BF16), preferred_element_type=F32)
        lgp[k] = part.astype(BF16)
        return carry

    lax.fori_loop(0, 2, reorder, 0)
    ys[0].wait_send()
    ys[1].wait_send()
    ys[2].start()
    ys[3].start()
    for i in range(3):
        ps[i].wait_recv()
    ps[3].start()
    lax.fori_loop(2, 4, reorder, 0)

    def stats(k, carry):
        part = lgp[k].astype(F32)
        top_k = jnp.max(part, axis=0, keepdims=True)
        stl[k, 0:1, :] = top_k
        stl[k, 1:2, :] = jnp.sum(jnp.exp(part - top_k), axis=0, keepdims=True)
        return carry

    lax.fori_loop(0, 4, stats, 0)

    def merged(buf):
        top = jnp.max(buf[:, 0, :], axis=0, keepdims=True)
        return top, jnp.sum(buf[:, 1, :] * jnp.exp(buf[:, 0, :] - top), axis=0, keepdims=True)

    def others(t):
        return y * 4 + (q + t) % 4

    s1 = [remote(stl.at[(q + t) % 4], s1b.at[q], s1_s.at[0], s1_r.at[0], (c, others(t))) for t in range(1, 4)]

    def s2_start(i, carry):
        remote(s1l, s2b.at[q, y], s2_s.at[0], s2_r.at[0], group(i)).start()
        return carry

    pltpu.make_async_copy(stl.at[q], s1b.at[q], s1_r.at[0]).start()
    for copy in s1:
        copy.start()

    ys[0].wait_recv()
    st[0] = (ry[0].astype(F32) + hb[A, rows_of(yr), :].astype(F32)).astype(BF16)
    ys[4].start()
    ys[1].wait_recv()
    st[1] = (ry[1].astype(F32) + hb[B, rows_of(yl), :].astype(F32)).astype(BF16)
    ys[5].start()

    def gather(buf, ss, rs):
        return [
            remote(buf.at[y, :, h], buf.at[y, :, h], ss.at[1], rs.at[1], right),
            remote(buf.at[y, :, h], buf.at[y, :, h], ss.at[2], rs.at[2], left),
            remote(buf.at[yl, 0, h], buf.at[yl, 0, h], ss.at[3], rs.at[3], right),
            remote(buf.at[yr, 1, h], buf.at[yr, 1, h], ss.at[4], rs.at[4], left),
            remote(buf.at[:, :, h], buf.at[:, :, h], ss.at[5], rs.at[5], mate),
        ]

    o_g = gather(ob, o_s, o_r)
    loads[4].wait()
    loads[5].wait()
    for i in range(16):
        xf[4 * i : 4 * i + 4, :] = xin[i].astype(F32)
    xin_b = xf[...].astype(BF16)

    def slope(i, carry):
        part = pl.ds(pl.multiple_of(i * 512, 512), 512)
        hid = jnp.dot(xin_b, win[:, part], preferred_element_type=F32)
        gp[:, part] = gelu_slope(hid)
        return carry

    lax.fori_loop(0, 3, slope, 0)
    pltpu.make_async_copy(s1b, s1b, s1_r.at[0]).wait()
    ps[3].wait_recv()
    ps[4].start()
    ps[5].start()
    s1l[0:1, :], s1l[1:2, :] = merged(s1b)
    pltpu.make_async_copy(s1l, s2b.at[q, y], s2_r.at[0]).start()
    lax.fori_loop(1, 16, s2_start, 0)
    lax.fori_loop(3, 6, slope, 0)

    ys[4].wait_send()
    ys[5].wait_send()
    z_o.wait_recv()
    o_g[0].start()
    o_g[1].start()
    ys[3].wait_recv()
    ys[4].wait_recv()
    qf[0:8] = hb[A, rows_of(y), :].astype(F32) + ry[3].astype(F32) + ry[4].astype(F32)
    ys[2].wait_recv()
    ys[5].wait_recv()
    qf[8:16] = hb[B, rows_of(y), :].astype(F32) + ry[2].astype(F32) + ry[5].astype(F32)
    for i in range(4):
        a2s[:, i] = qf[:, 4 * i : 4 * i + 4, :].astype(BF16)

    def a_start(cd, t):
        remote(a2s.at[cd, t], a2r.at[c * 4 + q], a_s.at[0], a_r.at[0], (cd, y * 4 + t)).start()

    pltpu.make_async_copy(a2s.at[c, q], a2r.at[c * 4 + q], a_r.at[0]).start()
    to_plane(a_start)

    loads[7].wait()
    pltpu.make_async_copy(s2b, s2b, s2_r.at[0]).wait()

    def xc_copy(i, k):
        return remote(xp.at[k, :, other], xrp.at[k], xc_s.at[0], xc_r.at[i], mate)

    def disp(i, carry):
        k = (y + 2 + i) % 4
        top, total = merged(s2b.at[k])
        d = jnp.exp(lgp[k].astype(F32) - top) * (1.0 / total)
        dspf[k] = d
        lw[k, :, 0:256] = d.astype(BF16)
        xp[k] = lax.dot_general(lw[k, :, 0:256], tok[...], TN, preferred_element_type=F32).astype(BF16)
        xc_copy(i, k).start()
        return carry

    lax.fori_loop(0, 4, disp, 0)

    o_g[0].wait_recv()
    o_g[2].start()
    o_g[1].wait_recv()
    o_g[3].start()

    def x_half(i, carry):
        k = (y + 2 + i) % 4
        xc_copy(i, k).wait_recv()
        hx[k] = (xp[k, :, mine].astype(F32) + xrp[k].astype(F32)).astype(BF16)
        return carry

    lax.fori_loop(0, 4, x_half, 0)
    XA, XB = pl.ds(0, 128), pl.ds(128, 128)

    def x_copy(i, src, dev):
        return remote(src, xry.at[i], x_s.at[0], x_r.at[i], dev)

    xs = [
        x_copy(0, hx.at[y2, XA], right),
        x_copy(1, hx.at[y2, XB], left),
        x_copy(2, hx.at[yr, XB], right),
        x_copy(3, hx.at[yl, XA], left),
        x_copy(4, xst.at[0], right),
        x_copy(5, xst.at[1], left),
    ]
    xs[0].start()
    xs[1].start()
    ps[4].wait_recv()
    ps[6].start()
    ps[5].wait_recv()
    ps[7].start()

    loads[6].wait()
    pltpu.make_async_copy(a2r, a2r, a_r.at[0]).wait()
    for i in range(16):
        for j in range(2):
            xf[4 * i : 4 * i + 4, 384 * j : 384 * j + 384] = (
                a2r[4 * i + j].astype(F32) + a2r[4 * i + 2 + j].astype(F32)
            )
    x_b = xf[...].astype(BF16)

    def act(i, carry):
        part = pl.ds(pl.multiple_of(i * 1024, 1024), 1024)
        a = lax.dot_general(x_b, wout[part, :], NT, preferred_element_type=F32)
        hc[:, part] = (a * gp[:, part]).astype(BF16)
        return carry

    lax.fori_loop(0, 3, act, 0)
    xs[2].start()
    xs[3].start()
    o_g[2].wait_recv()
    o_g[3].wait_recv()
    o_g[4].start()

    def grad(i, carry):
        part = pl.ds(pl.multiple_of(i * 256, 256), 256)
        xf[:, part] = lax.dot_general(hc[...], win[part, :], NT, preferred_element_type=F32)
        return carry

    lax.fori_loop(0, 3, grad, 0)
    for i in range(16):
        for j in range(2):
            b2s[i, j] = xf[4 * i : 4 * i + 4, 384 * j : 384 * j + 384].astype(BF16)

    def b_start(cd, t):
        remote(b2s.at[cd, t % 2], b2r.at[c * 4 + q], b_s.at[0], b_r.at[0], (cd, y * 4 + t)).start()

    pltpu.make_async_copy(b2s.at[c, h], b2r.at[c * 4 + q], b_r.at[0]).start()
    to_plane(b_start)

    xs[0].wait_recv()
    xst[0] = (xry[0].astype(F32) + hx[yr, XA, :].astype(F32)).astype(BF16)
    xs[4].start()
    xs[1].wait_recv()
    xst[1] = (xry[1].astype(F32) + hx[yl, XB, :].astype(F32)).astype(BF16)
    xs[5].start()
    ps[6].wait_recv()
    ps[7].wait_recv()
    ps[8].start()
    o_g[4].wait_recv()

    def comb_dot(i, carry):
        cols = pl.ds(pl.multiple_of(i * 256, 256), 256)
        w = ob[i].reshape(256, 768)
        cc[:, cols] = lax.dot_general(og[...], w, NT, preferred_element_type=F32)
        return carry

    lax.fori_loop(0, 4, comb_dot, 0)

    def comb_grad(i, carry):
        rows = pl.ds(pl.multiple_of(i * 64, 64), 64)
        comb = cf[rows, :]
        v = cc[rows, :]
        cb[rows, :] = (comb * (v - jnp.sum(comb * v, axis=1, keepdims=True))).astype(BF16)
        return carry

    lax.fori_loop(0, 8, comb_grad, 0)
    ps[8].wait_recv()

    def comb_out(i, carry):
        cols = pl.ds(pl.multiple_of(i * 256, 256), 256)
        w = sp[1, :, :, cols].reshape(1024, 256)
        acc[:, cols] = jnp.dot(cb[...], w, preferred_element_type=F32)
        return carry

    lax.fori_loop(0, 3, comb_out, 0)
    for i in range(2, 6):
        xs[i].wait_recv()
    xq[XA, :] = hx[y, XA, :].astype(F32) + xry[3].astype(F32) + xry[4].astype(F32)
    xq[XB, :] = hx[y, XB, :].astype(F32) + xry[2].astype(F32) + xry[5].astype(F32)

    pltpu.make_async_copy(b2r, b2r, b_r.at[0]).wait()
    back = b2r[...].reshape(16, 4, 4, 384)
    for i in range(4):
        zf[:, 4 * i : 4 * i + 4, :] = back[:, i].astype(F32)
    sgb[:, rows_of(y), mine] = zf[...].astype(BF16)

    def g_copy(i, part, yy, dev):
        ref = sgb.at[part, rows_of(yy), mine]
        return remote(ref, ref, g_s.at[min(i, 2)], g_r.at[i], dev)

    def k_copy(i, part, yy):
        ref = sgb.at[part, rows_of(yy), mine]
        return remote(ref, ref, k_s.at[0], k_r.at[i], mate)

    gs = [
        g_copy(0, A, y, right),
        g_copy(1, B, y, left),
        g_copy(2, B, y, right),
        g_copy(3, A, y, left),
        g_copy(4, A, yl, right),
        g_copy(5, B, yr, left),
    ]
    ks = [
        k_copy(0, A, y),
        k_copy(1, B, y),
        k_copy(2, A, yl),
        k_copy(3, B, yr),
        k_copy(4, B, yl),
        k_copy(5, A, yr),
        k_copy(6, A, y2),
        k_copy(7, B, y2),
    ]
    gs[0].start()
    gs[1].start()
    ks[0].start()
    ks[1].start()

    prod = zf[...].reshape(256, 384) * xq[...]
    ones = jnp.ones((8, 384), F32)
    dots = lax.dot_general(ones, prod, NT, precision=lax.Precision.HIGHEST, preferred_element_type=F32)
    dtl[...] = dots[0:1, :]

    def dt_copy(i):
        return remote(dtl, dtb.at[s], dt_s.at[0], dt_r.at[0], group(i))

    pltpu.make_async_copy(dtl, dtb.at[s], dt_r.at[0]).start()

    def dt_start(i, carry):
        dt_copy(i).start()
        return carry

    lax.fori_loop(1, 16, dt_start, 0)
    gs[0].wait_send()
    gs[1].wait_send()
    gs[2].start()
    gs[3].start()
    gs[0].wait_recv()
    gs[4].start()
    ks[2].start()
    gs[1].wait_recv()
    gs[5].start()
    ks[3].start()
    pltpu.make_async_copy(dtb, dtb, dt_r.at[0]).wait()

    def use(yy):
        w = sgb[:, rows_of(yy), :].reshape(256, 768)
        d = lax.dot_general(tok[...], w, NT, preferred_element_type=F32)
        lw[yy, :, 256:512] = (dspf[yy] * (d - jnp.sum(dtb[pl.ds(yy * 4, 4)], axis=0))).astype(BF16)
        both = sp[:, :, rows_of(yy), :].reshape(512, 768)
        return jnp.dot(lw[yy], both, preferred_element_type=F32)

    def add(yy):
        acc[...] += use(yy)

    ks[0].wait_recv()
    ks[1].wait_recv()
    add(y)
    gs[2].wait_recv()
    ks[4].start()
    gs[3].wait_recv()
    ks[5].start()
    ks[2].wait_recv()
    ks[4].wait_recv()
    add(yl)
    gs[4].wait_recv()
    ks[6].start()
    gs[5].wait_recv()
    ks[7].start()
    ks[3].wait_recv()
    ks[5].wait_recv()
    add(yr)
    ks[6].wait_recv()
    ks[7].wait_recv()
    out_ref[0] = (acc[...] + use(y2)).astype(BF16)

    for copy in ys[2:4] + o_g + ps + [z_o]:
        copy.wait_send()

    def drain(buf_src, sem):
        pltpu.make_async_copy(buf_src, buf_src, sem).wait()

    drain(rp, cs_s.at[0])
    drain(rp, xc_s.at[0])
    drain(rp, k_s.at[0])
    drain(rp.at[pl.ds(0, 12)], x_s.at[0])
    drain(rp.at[pl.ds(0, 8)], g_s.at[2])
    drain(a2r.at[pl.ds(0, 63)], a_s.at[0])
    drain(b2r.at[pl.ds(0, 63)], b_s.at[0])
    drain(s1b.at[pl.ds(0, 3)], s1_s.at[0])
    drain(s2b.reshape(16, 2, 256).at[pl.ds(0, 15)], s2_s.at[0])
    drain(dtb.at[pl.ds(0, 15)], dt_s.at[0])


def on_device(tokens, out_grad, saved_logits, slot_params, slot_inputs, slot_outputs, expert_in, expert_out):
    any_spec = pl.BlockSpec(memory_space=pl.ANY)
    vm = pltpu.VMEM
    dma = pltpu.SemaphoreType.DMA
    return pl.pallas_call(
        kernel,
        out_shape=pltpu.VMEM((1, 512, 768), BF16),
        in_specs=[any_spec] * 8,
        out_specs=pl.BlockSpec(memory_space=pltpu.VMEM),
        scratch_shapes=[
            vm((512, 1024), BF16),
            vm((512, 768), BF16),
            vm((512, 768), BF16),
            vm((768, 3072), BF16),
            vm((3072, 768), BF16),
            vm((16, 4, 768), BF16),
            vm((512, 1024), F32),
            vm((512, 1024), BF16),
            vm((16, 64, 768), BF16),
            vm((16, 64, 384), BF16),
            vm((16, 64, 384), BF16),
            vm((6, 8, 16, 384), BF16),
            vm((2, 8, 16, 384), BF16),
            vm((16, 16, 384), F32),
            vm((16, 4, 4, 384), BF16),
            vm((64, 4, 384), BF16),
            vm((64, 768), F32),
            vm((64, 3072), F32),
            vm((64, 3072), BF16),
            vm((16, 2, 4, 384), BF16),
            vm((64, 4, 384), BF16),
            vm((16, 16, 384), F32),
            vm((2, 16, 64, 768), BF16),
            vm((4, 2, 2, 64, 768), BF16),
            vm((512, 1024), F32),
            vm((4, 512, 256), F32),
            vm((4, 512, 512), BF16),
            vm((4, 2, 256), F32),
            vm((4, 2, 256), F32),
            vm((2, 256), F32),
            vm((4, 4, 2, 256), F32),
            vm((1, 256), F32),
            vm((16, 1, 256), F32),
            vm((512, 768), F32),
            vm((4, 512, 256), BF16),
            vm((4, 256, 768), BF16),
            vm((4, 256, 384), BF16),
            vm((4, 256, 384), BF16),
            vm((6, 128, 384), BF16),
            vm((2, 128, 384), BF16),
            vm((256, 384), F32),
            dma((8,)),
            dma((1,)), dma((4,)),
            dma((6,)), dma((6,)),
            dma((1,)), dma((1,)),
            dma((1,)), dma((1,)),
            dma((3,)), dma((6,)),
            dma((1,)), dma((8,)),
            dma((6,)), dma((6,)),
            dma((9,)), dma((9,)),
            dma((1,)), dma((1,)),
            dma((1,)), dma((1,)),
            dma((1,)), dma((1,)),
            dma((1,)), dma((4,)),
            dma((1,)), dma((6,)),
        ],
        compiler_params=pltpu.CompilerParams(
            collective_id=0, has_side_effects=True, vmem_limit_bytes=60 * 1024 * 1024
        ),
    )(tokens, out_grad, saved_logits, slot_params.T, slot_inputs, slot_outputs, expert_in, expert_out)


def solution(mesh):
    placed = (
        P("clip", "seq", None),
        P("clip", "seq", None),
        P("clip", "seq", None),
        P(None, "seq"),
        P(None, ("clip", "seq"), None),
        P("clip", "seq", None),
        P(("clip", "seq"), None, None),
        P(("clip", "seq"), None, None),
    )
    return jax.shard_map(
        on_device, mesh=mesh, in_specs=placed, out_specs=P("clip", "seq", None), check_vma=False
    )
```

```python
import jax
import jax.numpy as jnp
from jax import lax
from jax.experimental import pallas as pl
from jax.experimental.pallas import tpu as pltpu
from jax.sharding import PartitionSpec as P

F32 = jnp.float32
BF16 = jnp.bfloat16
MESH = pl.DeviceIdType.MESH
NT = (((1,), (1,)), ((), ()))
TN = (((0,), (0,)), ((), ()))


def gelu_slope(x):
    k = 0.7978845608028654
    t = jnp.tanh(k * (x + 0.044715 * x * x * x))
    return 0.5 * (1.0 + t) + 0.5 * x * (1.0 - t * t) * (k * (1.0 + 0.134145 * x * x))


def kernel(
    tok_h, og_h, lg_h, pt_h, xin_h, so_h, win_h, wout_h, out_ref,
    lg, og, tok, win, wout, xin, cf, cb, pb, rp, hb, ry, st, qf, a2s, a2r, xf, gp, hc, b2s, b2r, zf, sp,
    ob, cc, dspf, lw, stl, s1b, s1l, s2b, dtl, dtb, acc, lgp, xp, xrp, hx, xry, xst, xq,
    lg_s, ld, cs_s, cs_r, y_s, y_r, a_s, a_r, b_s, b_r, g_s, g_r, k_s, k_r, o_s, o_r, p_s, p_r, s1_s, s1_r, s2_s, s2_r, dt_s, dt_r, xc_s, xc_r, x_s, x_r,
):
    sgb, ptx = sp.at[0], sp.at[1].reshape(4, 2, 2, 4, 16, 768)
    c = lax.axis_index("clip")
    s = lax.axis_index("seq")
    y, q, h = s // 4, s % 4, s % 2
    zl = q // 2
    x, zh = c // 4, c % 4
    xr, xl = (x + 1) % 4, (x + 3) % 4
    yr, y2, yl = (y + 1) % 4, (y + 2) % 4, (y + 3) % 4
    right, left = (c, yr * 4 + q), (c, yl * 4 + q)
    mate = (c, s + 1 - 2 * h)
    zmate = (c, s + 2 - 4 * zl)
    mine = pl.ds(pl.multiple_of(h * 384, 128), 384)
    other = pl.ds(pl.multiple_of((1 - h) * 384, 128), 384)

    def rows_of(yy):
        return pl.ds(pl.multiple_of(yy * 16, 16), 16)

    def drain(ref, sem):
        pltpu.make_async_copy(ref, ref, sem).wait()

    two = rp.at[pl.ds(0, 4)]

    def remote(src, dst, ssem, rsem, dev):
        return pltpu.make_async_remote_copy(
            src_ref=src, dst_ref=dst, send_sem=ssem, recv_sem=rsem, device_id=dev, device_id_type=MESH
        )

    def far(k):
        return ((c // 4 + 3 - k // 4) % 4) * 4 + (c + 3 - k % 4) % 4

    def to_plane(send):
        def step(k, carry):
            for t in range(4):
                send(far(k), t)
            return carry

        lax.fori_loop(0, 15, step, 0)
        for t in range(1, 4):
            send(c, (q + t) % 4)

    def group(i):
        return (c, (s + i) % 16)

    loads = [
        None,
        pltpu.make_async_copy(og_h.at[0], og, ld.at[1]),
        pltpu.make_async_copy(so_h.at[0], ob.at[y, zl, h], ld.at[2]),
        pltpu.make_async_copy(pt_h.at[rows_of(x)], ptx.at[y, zl, h, x], ld.at[3]),
        pltpu.make_async_copy(xin_h, xin, ld.at[4]),
        pltpu.make_async_copy(win_h.at[0], win, ld.at[5]),
        pltpu.make_async_copy(wout_h.at[0], wout, ld.at[6]),
        pltpu.make_async_copy(tok_h.at[0], tok, ld.at[7]),
    ]
    lg_loads = [
        pltpu.make_async_copy(lg_h.at[0, pl.ds(256 * i, 256)], lg.at[pl.ds(256 * i, 256)], lg_s.at[i]) for i in range(2)
    ]
    for load in lg_loads:
        load.start()
    loads[1].start()

    barrier = pltpu.get_barrier_semaphore()

    def greet_plane(cd, t):
        pl.semaphore_signal(barrier, inc=1, device_id=(cd, y * 4 + t), device_id_type=MESH)

    def greet_group(i, carry):
        pl.semaphore_signal(
            barrier, inc=1, device_id=(c, ((y + 1 + i // 4) % 4) * 4 + i % 4), device_id_type=MESH
        )
        return carry

    to_plane(greet_plane)
    lax.fori_loop(0, 12, greet_group, 0)

    def front(i, carry):
        rows = pl.ds(pl.multiple_of(i * 64, 64), 64)
        l = lg[rows, :].astype(F32)
        e = jnp.exp(l - jnp.max(l, axis=1, keepdims=True))
        comb = e * (1.0 / jnp.sum(e, axis=1, keepdims=True))
        cf[rows, :] = comb
        cb[rows, :] = comb.astype(BF16)
        return carry

    for i in range(2):
        lg_loads[i].wait()
        lax.fori_loop(4 * i, 4 * i + 4, front, 0, unroll=2)
        if i == 0:
            for load in loads[2:]:
                load.start()
    loads[1].wait()

    def cs_copy(i):
        part = rows_of((y + 2 + i) % 4)
        return remote(pb.at[:, part, other], rp.at[:, part], cs_s.at[0], cs_r.at[i], mate)

    def partial(k, carry):
        cols = pl.ds(pl.multiple_of(k * 256, 256), 256)
        p = lax.dot_general(cb[:, cols], og[...], TN, preferred_element_type=F32)
        pb[pl.ds(k * 4, 4)] = p.astype(BF16).reshape(4, 64, 768)
        return carry

    lax.fori_loop(0, 4, partial, 0)
    pl.semaphore_wait(barrier, 75)
    for i in range(4):
        cs_copy(i).start()

    def p_copy(i, ref, dev):
        return remote(ref, ref, p_s.at[0], p_r.at[(0, 0, 0, 1, 2, 2, 3, 3, 4)[i]], dev)

    x_right, x_left = (xr * 4 + zh, s), (xl * 4 + zh, s)
    ps = [
        p_copy(0, ptx.at[y, zl, h, x], right),
        p_copy(1, ptx.at[y, zl, h, x], left),
        p_copy(2, ptx.at[y, zl, h, x], (c, y2 * 4 + q)),
        p_copy(3, ptx.at[:, zl, h, x], zmate),
        p_copy(4, ptx.at[:, :, h, x], x_right),
        p_copy(5, ptx.at[:, :, h, x], x_left),
        p_copy(6, ptx.at[:, 0, h, xl], x_right),
        p_copy(7, ptx.at[:, 1, h, xr], x_left),
        p_copy(8, ptx.at[:, :, h], mate),
    ]
    loads[2].wait()
    loads[3].wait()
    z_o = remote(ob.at[y, zl, h], ob.at[y, zl, h], o_s.at[0], o_r.at[0], zmate)
    z_o.start()
    for i in range(3):
        ps[i].start()

    def half_sum(i):
        part = rows_of((y + 2 + i) % 4)
        cs_copy(i).wait_recv()
        hb[:, part, :] = (pb[:, part, mine].astype(F32) + rp[:, part, :].astype(F32)).astype(BF16)

    A, B = pl.ds(0, 8), pl.ds(8, 8)

    def y_copy(i, src, dev):
        return remote(src, ry.at[i], y_s.at[i // 2], y_r.at[(0, 1, 3, 2, 2, 3)[i]], dev)

    ys = [
        y_copy(0, hb.at[A, rows_of(y2)], right),
        y_copy(1, hb.at[B, rows_of(y2)], left),
        y_copy(2, hb.at[B, rows_of(yr)], right),
        y_copy(3, hb.at[A, rows_of(yl)], left),
        y_copy(4, st.at[0], right),
        y_copy(5, st.at[1], left),
    ]
    half_sum(0)
    ys[0].start()
    ys[1].start()
    for i in range(1, 4):
        half_sum(i)

    def reorder(k, carry):
        p = lax.broadcasted_iota(jnp.int32, (1, 256), 1)
        pick = lax.broadcasted_iota(jnp.int32, (1024, 256), 0) == (p // 16) * 64 + p % 16 + k * 16
        part = jnp.dot(lg[...], pick.astype(F32).astype(BF16), preferred_element_type=F32)
        lgp[k] = part.astype(BF16)
        return carry

    lax.fori_loop(0, 2, reorder, 0)
    drain(two, y_s.at[0])
    ys[2].start()
    ys[3].start()
    ptf = sp.at[1].reshape(64, 16, 768)
    drain(ptf.at[pl.ds(0, 3)], p_r.at[0])
    ps[3].start()
    lax.fori_loop(2, 4, reorder, 0)

    def stats(k, carry):
        part = lgp[k].astype(F32)
        top_k = jnp.max(part, axis=0, keepdims=True)
        stl[k, 0:1, :] = top_k
        stl[k, 1:2, :] = jnp.sum(jnp.exp(part - top_k), axis=0, keepdims=True)
        return carry

    lax.fori_loop(0, 4, stats, 0)

    def merged(buf):
        top = jnp.max(buf[:, 0, :], axis=0, keepdims=True)
        return top, jnp.sum(buf[:, 1, :] * jnp.exp(buf[:, 0, :] - top), axis=0, keepdims=True)

    def others(t):
        return y * 4 + (q + t) % 4

    s1 = [remote(stl.at[(q + t) % 4], s1b.at[q], s1_s.at[0], s1_r.at[0], (c, others(t))) for t in range(1, 4)]

    def s2_start(i, carry):
        remote(s1l, s2b.at[q, y], s2_s.at[0], s2_r.at[0], group(i)).start()
        return carry

    pltpu.make_async_copy(stl.at[q], s1b.at[q], s1_r.at[0]).start()
    for copy in s1:
        copy.start()

    ys[0].wait_recv()
    st[0] = (ry[0].astype(F32) + hb[A, rows_of(yr), :].astype(F32)).astype(BF16)
    ys[4].start()
    ys[1].wait_recv()
    st[1] = (ry[1].astype(F32) + hb[B, rows_of(yl), :].astype(F32)).astype(BF16)
    ys[5].start()

    def gather(buf, ss, rs):
        return [
            remote(buf.at[y, :, h], buf.at[y, :, h], ss.at[0], rs.at[1], right),
            remote(buf.at[y, :, h], buf.at[y, :, h], ss.at[0], rs.at[1], left),
            remote(buf.at[yl, 0, h], buf.at[yl, 0, h], ss.at[0], rs.at[2], right),
            remote(buf.at[yr, 1, h], buf.at[yr, 1, h], ss.at[0], rs.at[2], left),
            remote(buf.at[:, :, h], buf.at[:, :, h], ss.at[0], rs.at[3], mate),
        ]

    o_g = gather(ob, o_s, o_r)
    loads[4].wait()
    loads[5].wait()
    for i in range(16):
        xf[4 * i : 4 * i + 4, :] = xin[i].astype(F32)
    xin_b = xf[...].astype(BF16)

    def slope(i, carry):
        part = pl.ds(pl.multiple_of(i * 512, 512), 512)
        hid = jnp.dot(xin_b, win[:, part], preferred_element_type=F32)
        gp[:, part] = gelu_slope(hid)
        return carry

    lax.fori_loop(0, 3, slope, 0)
    pltpu.make_async_copy(s1b, s1b, s1_r.at[0]).wait()
    ps[3].wait_recv()
    ps[4].start()
    ps[5].start()
    s1l[0:1, :], s1l[1:2, :] = merged(s1b)
    pltpu.make_async_copy(s1l, s2b.at[q, y], s2_r.at[0]).start()
    lax.fori_loop(1, 16, s2_start, 0)
    lax.fori_loop(3, 6, slope, 0)

    drain(two, y_s.at[2])
    z_o.wait_recv()
    o_g[0].start()
    o_g[1].start()
    drain(two, y_r.at[2])
    qf[0:8] = hb[A, rows_of(y), :].astype(F32) + ry[3].astype(F32) + ry[4].astype(F32)
    drain(two, y_r.at[3])
    qf[8:16] = hb[B, rows_of(y), :].astype(F32) + ry[2].astype(F32) + ry[5].astype(F32)
    for i in range(4):
        a2s[:, i] = qf[:, 4 * i : 4 * i + 4, :].astype(BF16)

    def a_start(cd, t):
        remote(a2s.at[cd, t], a2r.at[c * 4 + q], a_s.at[0], a_r.at[0], (cd, y * 4 + t)).start()

    pltpu.make_async_copy(a2s.at[c, q], a2r.at[c * 4 + q], a_r.at[0]).start()
    to_plane(a_start)

    loads[7].wait()
    pltpu.make_async_copy(s2b, s2b, s2_r.at[0]).wait()

    def xc_copy(i, k):
        return remote(xp.at[k, :, other], xrp.at[k], xc_s.at[0], xc_r.at[0], mate)

    def disp(i, carry):
        k = (y + 2 + i) % 4
        top, total = merged(s2b.at[k])
        d = jnp.exp(lgp[k].astype(F32) - top) * (1.0 / total)
        dspf[k] = d
        lw[k, :, 0:256] = d.astype(BF16)
        xp[k] = lax.dot_general(lw[k, :, 0:256], tok[...], TN, preferred_element_type=F32).astype(BF16)
        xc_copy(i, k).start()
        return carry

    lax.fori_loop(0, 4, disp, 0)

    obf = ob.reshape(16, 64, 768)
    drain(obf.at[pl.ds(0, 4)], o_r.at[1])
    o_g[2].start()
    o_g[3].start()

    def x_half(i, carry):
        k = (y + 2 + i) % 4
        hx[k] = (xp[k, :, mine].astype(F32) + xrp[k].astype(F32)).astype(BF16)
        return carry

    drain(xrp, xc_r.at[0])
    lax.fori_loop(0, 4, x_half, 0)
    XA, XB = pl.ds(0, 128), pl.ds(128, 128)

    def x_copy(i, src, dev):
        return remote(src, xry.at[i], x_s.at[0], x_r.at[i // 2 if i < 2 else 1], dev)

    xs = [
        x_copy(0, hx.at[y2, XA], right),
        x_copy(1, hx.at[y2, XB], left),
        x_copy(2, hx.at[yr, XB], right),
        x_copy(3, hx.at[yl, XA], left),
        x_copy(4, xst.at[0], right),
        x_copy(5, xst.at[1], left),
    ]
    xs[0].start()
    xs[1].start()
    drain(ptf.at[pl.ds(0, 16)], p_r.at[2])
    ps[6].start()
    ps[7].start()

    loads[6].wait()
    pltpu.make_async_copy(a2r, a2r, a_r.at[0]).wait()
    for i in range(16):
        for j in range(2):
            xf[4 * i : 4 * i + 4, 384 * j : 384 * j + 384] = (
                a2r[4 * i + j].astype(F32) + a2r[4 * i + 2 + j].astype(F32)
            )
    x_b = xf[...].astype(BF16)

    def act(i, carry):
        part = pl.ds(pl.multiple_of(i * 1024, 1024), 1024)
        a = lax.dot_general(x_b, wout[part, :], NT, preferred_element_type=F32)
        hc[:, part] = (a * gp[:, part]).astype(BF16)
        return carry

    lax.fori_loop(0, 3, act, 0)
    xs[2].start()
    xs[3].start()
    drain(obf.at[pl.ds(0, 2)], o_r.at[2])
    o_g[4].start()

    def grad(i, carry):
        part = pl.ds(pl.multiple_of(i * 256, 256), 256)
        xf[:, part] = lax.dot_general(hc[...], win[part, :], NT, preferred_element_type=F32)
        return carry

    lax.fori_loop(0, 3, grad, 0)
    for i in range(16):
        for j in range(2):
            b2s[i, j] = xf[4 * i : 4 * i + 4, 384 * j : 384 * j + 384].astype(BF16)

    def b_start(cd, t):
        remote(b2s.at[cd, t % 2], b2r.at[c * 4 + q], b_s.at[0], b_r.at[0], (cd, y * 4 + t)).start()

    pltpu.make_async_copy(b2s.at[c, h], b2r.at[c * 4 + q], b_r.at[0]).start()
    to_plane(b_start)

    drain(two, x_r.at[0])
    xst[0] = (xry[0].astype(F32) + hx[yr, XA, :].astype(F32)).astype(BF16)
    xs[4].start()
    xst[1] = (xry[1].astype(F32) + hx[yl, XB, :].astype(F32)).astype(BF16)
    xs[5].start()
    drain(ptf.at[pl.ds(0, 8)], p_r.at[3])
    ps[8].start()
    o_g[4].wait_recv()

    def comb_dot(i, carry):
        cols = pl.ds(pl.multiple_of(i * 256, 256), 256)
        w = ob[i].reshape(256, 768)
        cc[:, cols] = lax.dot_general(og[...], w, NT, preferred_element_type=F32)
        return carry

    lax.fori_loop(0, 4, comb_dot, 0)

    def comb_grad(i, carry):
        rows = pl.ds(pl.multiple_of(i * 64, 64), 64)
        comb = cf[rows, :]
        v = cc[rows, :]
        cb[rows, :] = (comb * (v - jnp.sum(comb * v, axis=1, keepdims=True))).astype(BF16)
        return carry

    lax.fori_loop(0, 8, comb_grad, 0)
    ps[8].wait_recv()

    def comb_out(i, carry):
        cols = pl.ds(pl.multiple_of(i * 256, 256), 256)
        w = sp[1, :, :, cols].reshape(1024, 256)
        acc[:, cols] = jnp.dot(cb[...], w, preferred_element_type=F32)
        return carry

    lax.fori_loop(0, 3, comb_out, 0)
    drain(rp.at[pl.ds(0, 8)], x_r.at[1])
    xq[XA, :] = hx[y, XA, :].astype(F32) + xry[3].astype(F32) + xry[4].astype(F32)
    xq[XB, :] = hx[y, XB, :].astype(F32) + xry[2].astype(F32) + xry[5].astype(F32)

    pltpu.make_async_copy(b2r, b2r, b_r.at[0]).wait()
    back = b2r[...].reshape(16, 4, 4, 384)
    for i in range(4):
        zf[:, 4 * i : 4 * i + 4, :] = back[:, i].astype(F32)
    sgb[:, rows_of(y), mine] = zf[...].astype(BF16)

    def g_copy(i, part, yy, dev):
        ref = sgb.at[part, rows_of(yy), mine]
        return remote(ref, ref, g_s.at[min(i // 2, 1)], g_r.at[(0, 1, 2, 2, 3, 3)[i]], dev)

    def k_copy(i, part, yy):
        ref = sgb.at[part, rows_of(yy), mine]
        return remote(ref, ref, k_s.at[0], k_r.at[(0, 0, 1, 2, 1, 2, 3, 3)[i]], mate)

    gs = [
        g_copy(0, A, y, right),
        g_copy(1, B, y, left),
        g_copy(2, B, y, right),
        g_copy(3, A, y, left),
        g_copy(4, A, yl, right),
        g_copy(5, B, yr, left),
    ]
    ks = [
        k_copy(0, A, y),
        k_copy(1, B, y),
        k_copy(2, A, yl),
        k_copy(3, B, yr),
        k_copy(4, B, yl),
        k_copy(5, A, yr),
        k_copy(6, A, y2),
        k_copy(7, B, y2),
    ]
    gs[0].start()
    gs[1].start()
    ks[0].start()
    ks[1].start()

    prod = zf[...].reshape(256, 384) * xq[...]
    ones = jnp.ones((8, 384), F32)
    dots = lax.dot_general(ones, prod, NT, precision=lax.Precision.HIGHEST, preferred_element_type=F32)
    dtl[...] = dots[0:1, :]

    def dt_copy(i):
        return remote(dtl, dtb.at[s], dt_s.at[0], dt_r.at[0], group(i))

    pltpu.make_async_copy(dtl, dtb.at[s], dt_r.at[0]).start()

    def dt_start(i, carry):
        dt_copy(i).start()
        return carry

    lax.fori_loop(1, 16, dt_start, 0)
    drain(two, g_s.at[0])
    gs[2].start()
    gs[3].start()
    gs[0].wait_recv()
    gs[4].start()
    ks[2].start()
    gs[1].wait_recv()
    gs[5].start()
    ks[3].start()
    pltpu.make_async_copy(dtb, dtb, dt_r.at[0]).wait()

    def prepare(yy):
        w = sgb[:, rows_of(yy), :].reshape(256, 768)
        d = lax.dot_general(tok[...], w, NT, preferred_element_type=F32)
        lw[yy, :, 256:512] = (dspf[yy] * (d - jnp.sum(dtb[pl.ds(yy * 4, 4)], axis=0))).astype(BF16)

    def use(yy):
        return jnp.dot(lw[yy], sp[:, :, rows_of(yy), :].reshape(512, 768), preferred_element_type=F32)

    drain(two, k_r.at[0])
    prepare(y)
    acc[...] += use(y)
    drain(two, g_r.at[2])
    ks[4].start()
    ks[5].start()
    drain(two, k_r.at[1])
    prepare(yl)
    drain(two, g_r.at[3])
    ks[6].start()
    ks[7].start()
    acc[...] += use(yl)
    drain(two, k_r.at[2])
    prepare(yr)
    acc[...] += use(yr)
    drain(two, k_r.at[3])
    prepare(y2)
    out_ref[0] = (acc[...] + use(y2)).astype(BF16)

    drain(two, y_s.at[1])
    drain(obf.at[pl.ds(0, 15)], o_s.at[0])
    drain(ptf.at[pl.ds(0, 63)], p_s.at[0])
    drain(rp, cs_s.at[0])
    drain(rp, xc_s.at[0])
    drain(rp, k_s.at[0])
    drain(rp.at[pl.ds(0, 12)], x_s.at[0])
    drain(rp.at[pl.ds(0, 8)], g_s.at[1])
    drain(a2r.at[pl.ds(0, 63)], a_s.at[0])
    drain(b2r.at[pl.ds(0, 63)], b_s.at[0])
    drain(s1b.at[pl.ds(0, 3)], s1_s.at[0])
    drain(s2b.reshape(16, 2, 256).at[pl.ds(0, 15)], s2_s.at[0])
    drain(dtb.at[pl.ds(0, 15)], dt_s.at[0])


def on_device(tokens, out_grad, saved_logits, slot_params, slot_inputs, slot_outputs, expert_in, expert_out):
    any_spec = pl.BlockSpec(memory_space=pl.ANY)
    vm = pltpu.VMEM
    dma = pltpu.SemaphoreType.DMA
    return pl.pallas_call(
        kernel,
        out_shape=pltpu.VMEM((1, 512, 768), BF16),
        in_specs=[any_spec] * 8,
        out_specs=pl.BlockSpec(memory_space=pltpu.VMEM),
        scratch_shapes=[
            vm((512, 1024), BF16),
            vm((512, 768), BF16),
            vm((512, 768), BF16),
            vm((768, 3072), BF16),
            vm((3072, 768), BF16),
            vm((16, 4, 768), BF16),
            vm((512, 1024), F32),
            vm((512, 1024), BF16),
            vm((16, 64, 768), BF16),
            vm((16, 64, 384), BF16),
            vm((16, 64, 384), BF16),
            vm((6, 8, 16, 384), BF16),
            vm((2, 8, 16, 384), BF16),
            vm((16, 16, 384), F32),
            vm((16, 4, 4, 384), BF16),
            vm((64, 4, 384), BF16),
            vm((64, 768), F32),
            vm((64, 3072), F32),
            vm((64, 3072), BF16),
            vm((16, 2, 4, 384), BF16),
            vm((64, 4, 384), BF16),
            vm((16, 16, 384), F32),
            vm((2, 16, 64, 768), BF16),
            vm((4, 2, 2, 64, 768), BF16),
            vm((512, 1024), F32),
            vm((4, 512, 256), F32),
            vm((4, 512, 512), BF16),
            vm((4, 2, 256), F32),
            vm((4, 2, 256), F32),
            vm((2, 256), F32),
            vm((4, 4, 2, 256), F32),
            vm((1, 256), F32),
            vm((16, 1, 256), F32),
            vm((512, 768), F32),
            vm((4, 512, 256), BF16),
            vm((4, 256, 768), BF16),
            vm((4, 256, 384), BF16),
            vm((4, 256, 384), BF16),
            vm((6, 128, 384), BF16),
            vm((2, 128, 384), BF16),
            vm((256, 384), F32),
            dma((2,)), dma((8,)),
            dma((1,)), dma((4,)),
            dma((3,)), dma((4,)),
            dma((1,)), dma((1,)),
            dma((1,)), dma((1,)),
            dma((2,)), dma((4,)),
            dma((1,)), dma((4,)),
            dma((1,)), dma((4,)),
            dma((1,)), dma((5,)),
            dma((1,)), dma((1,)),
            dma((1,)), dma((1,)),
            dma((1,)), dma((1,)),
            dma((1,)), dma((1,)),
            dma((1,)), dma((2,)),
        ],
        compiler_params=pltpu.CompilerParams(
            collective_id=0, has_side_effects=True, vmem_limit_bytes=60 * 1024 * 1024
        ),
    )(tokens, out_grad, saved_logits, slot_params.T, slot_inputs, slot_outputs, expert_in, expert_out)


def solution(mesh):
    placed = (
        P("clip", "seq", None),
        P("clip", "seq", None),
        P("clip", "seq", None),
        P(None, "seq"),
        P(None, ("clip", "seq"), None),
        P("clip", "seq", None),
        P(("clip", "seq"), None, None),
        P(("clip", "seq"), None, None),
    )
    return jax.shard_map(
        on_device, mesh=mesh, in_specs=placed, out_specs=P("clip", "seq", None), check_vma=False
    )
```

```python
import jax
import jax.numpy as jnp
from jax import lax
from jax.experimental import pallas as pl
from jax.experimental.pallas import tpu as pltpu
from jax.sharding import PartitionSpec as P

F32 = jnp.float32
BF16 = jnp.bfloat16
MESH = pl.DeviceIdType.MESH
NT = (((1,), (1,)), ((), ()))
TN = (((0,), (0,)), ((), ()))


def gelu_slope(x):
    k = 0.7978845608028654
    t = jnp.tanh(k * (x + 0.044715 * x * x * x))
    return 0.5 * (1.0 + t) + 0.5 * x * (1.0 - t * t) * (k * (1.0 + 0.134145 * x * x))


def kernel(
    tok_h, og_h, lg_h, pt_h, xin_h, so_h, win_h, wout_h, out_ref,
    lg, og, tok, win, wout, xin, cf, cb, pb, rp, hb, ry, st, qf, a2s, a2r, xf, gp, hc, b2s, b2r, zf, sp,
    ob, cc, dspf, lw, stl, s1b, s1l, s2b, dtl, dtb, acc, lgp, xp, xrp, hx, xry, xst, xq, dn,
    lg_s, ld, cs_s, cs_r, y_s, y_r, a_s, a_r, b_s, b_r, g_s, g_r, k_s, k_r, o_s, o_r, p_s, p_r, s1_s, s1_r, s2_s, s2_r, dt_s, dt_r, xc_s, xc_r, x_s, x_r,
):
    sgb, ptx = sp.at[0], sp.at[1].reshape(4, 2, 2, 4, 16, 768)
    c = lax.axis_index("clip")
    s = lax.axis_index("seq")
    y, q, h = s // 4, s % 4, s % 2
    zl = q // 2
    x, zh = c // 4, c % 4
    xr, xl = (x + 1) % 4, (x + 3) % 4
    yr, y2, yl = (y + 1) % 4, (y + 2) % 4, (y + 3) % 4
    right, left = (c, yr * 4 + q), (c, yl * 4 + q)
    mate = (c, s + 1 - 2 * h)
    zmate = (c, s + 2 - 4 * zl)
    mine = pl.ds(pl.multiple_of(h * 384, 128), 384)
    other = pl.ds(pl.multiple_of((1 - h) * 384, 128), 384)

    def rows_of(yy):
        return pl.ds(pl.multiple_of(yy * 16, 16), 16)

    def drain(ref, sem):
        pltpu.make_async_copy(ref, ref, sem).wait()

    two = rp.at[pl.ds(0, 4)]

    def remote(src, dst, ssem, rsem, dev):
        return pltpu.make_async_remote_copy(
            src_ref=src, dst_ref=dst, send_sem=ssem, recv_sem=rsem, device_id=dev, device_id_type=MESH
        )

    def far(k):
        return ((c // 4 + 3 - k // 4) % 4) * 4 + (c + 3 - k % 4) % 4

    def to_plane(send):
        def step(k, carry):
            for t in range(4):
                send(far(k), t)
            return carry

        lax.fori_loop(0, 15, step, 0)
        for t in range(1, 4):
            send(c, (q + t) % 4)

    def group(i):
        return (c, (s + i) % 16)

    loads = [
        None,
        pltpu.make_async_copy(og_h.at[0], og, ld.at[1]),
        pltpu.make_async_copy(so_h.at[0], ob.at[y, zl, h], ld.at[2]),
        pltpu.make_async_copy(pt_h.at[rows_of(x)], ptx.at[y, zl, h, x], ld.at[3]),
        pltpu.make_async_copy(xin_h, xin, ld.at[4]),
        pltpu.make_async_copy(win_h.at[0], win, ld.at[5]),
        pltpu.make_async_copy(wout_h.at[0], wout, ld.at[6]),
        pltpu.make_async_copy(tok_h.at[0], tok, ld.at[0]),
    ]
    lg_loads = [
        pltpu.make_async_copy(lg_h.at[0, pl.ds(256 * i, 256)], lg.at[pl.ds(256 * i, 256)], lg_s.at[i]) for i in range(2)
    ]
    for load in lg_loads:
        load.start()
    loads[1].start()

    barrier = pltpu.get_barrier_semaphore()

    def greet_plane(cd, t):
        pl.semaphore_signal(barrier, inc=1, device_id=(cd, y * 4 + t), device_id_type=MESH)

    def greet_group(i, carry):
        pl.semaphore_signal(
            barrier, inc=1, device_id=(c, ((y + 1 + i // 4) % 4) * 4 + i % 4), device_id_type=MESH
        )
        return carry

    to_plane(greet_plane)
    lax.fori_loop(0, 12, greet_group, 0)

    def front(i, carry):
        rows = pl.ds(pl.multiple_of(i * 64, 64), 64)
        l = lg[rows, :].astype(F32)
        e = jnp.exp(l - jnp.max(l, axis=1, keepdims=True))
        comb = e * (1.0 / jnp.sum(e, axis=1, keepdims=True))
        cf[rows, :] = comb
        cb[rows, :] = comb.astype(BF16)
        return carry

    for i in range(2):
        lg_loads[i].wait()
        lax.fori_loop(4 * i, 4 * i + 4, front, 0, unroll=2)
        if i == 0:
            for load in loads[2:]:
                load.start()
    loads[1].wait()

    def cs_copy(i):
        part = rows_of((y + 2 + i) % 4)
        return remote(pb.at[:, part, other], rp.at[:, part], cs_s.at[0], cs_r.at[i], mate)

    def partial(k, carry):
        cols = pl.ds(pl.multiple_of(k * 256, 256), 256)
        p = lax.dot_general(cb[:, cols], og[...], TN, preferred_element_type=F32)
        pb[pl.ds(k * 4, 4)] = p.astype(BF16).reshape(4, 64, 768)
        return carry

    lax.fori_loop(0, 4, partial, 0)
    pl.semaphore_wait(barrier, 75)
    for i in range(4):
        cs_copy(i).start()

    def p_copy(i, ref, dev):
        return remote(ref, ref, p_s.at[0], p_r.at[(0, 0, 0, 1, 2, 2, 3, 3, 4)[i]], dev)

    x_right, x_left = (xr * 4 + zh, s), (xl * 4 + zh, s)
    ps = [
        p_copy(0, ptx.at[y, zl, h, x], right),
        p_copy(1, ptx.at[y, zl, h, x], left),
        p_copy(2, ptx.at[y, zl, h, x], (c, y2 * 4 + q)),
        p_copy(3, ptx.at[:, zl, h, x], zmate),
        p_copy(4, ptx.at[:, :, h, x], x_right),
        p_copy(5, ptx.at[:, :, h, x], x_left),
        p_copy(6, ptx.at[:, 0, h, xl], x_right),
        p_copy(7, ptx.at[:, 1, h, xr], x_left),
        p_copy(8, ptx.at[:, :, h], mate),
    ]
    loads[2].wait()
    loads[3].wait()
    z_o = remote(ob.at[y, zl, h], ob.at[y, zl, h], o_s.at[0], o_r.at[0], zmate)
    z_o.start()
    for i in range(3):
        ps[i].start()

    def half_sum(i):
        part = rows_of((y + 2 + i) % 4)
        cs_copy(i).wait_recv()
        hb[:, part, :] = (pb[:, part, mine].astype(F32) + rp[:, part, :].astype(F32)).astype(BF16)

    A, B = pl.ds(0, 8), pl.ds(8, 8)

    def y_copy(i, src, dev):
        return remote(src, ry.at[i], y_s.at[i // 2], y_r.at[(0, 1, 3, 2, 2, 3)[i]], dev)

    ys = [
        y_copy(0, hb.at[A, rows_of(y2)], right),
        y_copy(1, hb.at[B, rows_of(y2)], left),
        y_copy(2, hb.at[B, rows_of(yr)], right),
        y_copy(3, hb.at[A, rows_of(yl)], left),
        y_copy(4, st.at[0], right),
        y_copy(5, st.at[1], left),
    ]
    half_sum(0)
    ys[0].start()
    ys[1].start()
    for i in range(1, 4):
        half_sum(i)

    def reorder(k, carry):
        p = lax.broadcasted_iota(jnp.int32, (1, 256), 1)
        pick = lax.broadcasted_iota(jnp.int32, (1024, 256), 0) == (p // 16) * 64 + p % 16 + k * 16
        part = jnp.dot(lg[...], pick.astype(F32).astype(BF16), preferred_element_type=F32)
        lgp[k] = part.astype(BF16)
        return carry

    lax.fori_loop(0, 2, reorder, 0)
    drain(two, y_s.at[0])
    ys[2].start()
    ys[3].start()
    ptf = sp.at[1].reshape(64, 16, 768)
    drain(ptf.at[pl.ds(0, 3)], p_r.at[0])
    ps[3].start()
    lax.fori_loop(2, 4, reorder, 0)

    def stats(k, carry):
        part = lgp[k].astype(F32)
        top_k = jnp.max(part, axis=0, keepdims=True)
        stl[k, 0:1, :] = top_k
        stl[k, 1:2, :] = jnp.sum(jnp.exp(part - top_k), axis=0, keepdims=True)
        return carry

    lax.fori_loop(0, 4, stats, 0)

    def merged(buf):
        top = jnp.max(buf[:, 0, :], axis=0, keepdims=True)
        return top, jnp.sum(buf[:, 1, :] * jnp.exp(buf[:, 0, :] - top), axis=0, keepdims=True)

    def others(t):
        return y * 4 + (q + t) % 4

    s1 = [remote(stl.at[(q + t) % 4], s1b.at[q], s1_s.at[0], s1_r.at[0], (c, others(t))) for t in range(1, 4)]

    def s2_start(i, carry):
        remote(s1l, s2b.at[q, y], s2_s.at[0], s2_r.at[0], group(i)).start()
        return carry

    pltpu.make_async_copy(stl.at[q], s1b.at[q], s1_r.at[0]).start()
    for copy in s1:
        copy.start()

    ys[0].wait_recv()
    st[0] = (ry[0].astype(F32) + hb[A, rows_of(yr), :].astype(F32)).astype(BF16)
    ys[4].start()
    ys[1].wait_recv()
    st[1] = (ry[1].astype(F32) + hb[B, rows_of(yl), :].astype(F32)).astype(BF16)
    ys[5].start()

    def gather(buf, ss, rs):
        return [
            remote(buf.at[y, :, h], buf.at[y, :, h], ss.at[0], rs.at[1], right),
            remote(buf.at[y, :, h], buf.at[y, :, h], ss.at[0], rs.at[1], left),
            remote(buf.at[yl, 0, h], buf.at[yl, 0, h], ss.at[0], rs.at[2], right),
            remote(buf.at[yr, 1, h], buf.at[yr, 1, h], ss.at[0], rs.at[2], left),
            remote(buf.at[:, :, h], buf.at[:, :, h], ss.at[0], rs.at[3], mate),
        ]

    o_g = gather(ob, o_s, o_r)
    loads[4].wait()
    loads[5].wait()
    for i in range(16):
        xf[4 * i : 4 * i + 4, :] = xin[i].astype(F32)
    xin_b = xf[...].astype(BF16)

    def slope(i, carry):
        part = pl.ds(pl.multiple_of(i * 512, 512), 512)
        hid = jnp.dot(xin_b, win[:, part], preferred_element_type=F32)
        gp[:, part] = gelu_slope(hid)
        return carry

    lax.fori_loop(0, 3, slope, 0)
    pltpu.make_async_copy(s1b, s1b, s1_r.at[0]).wait()
    ps[3].wait_recv()
    ps[4].start()
    ps[5].start()
    s1l[0:1, :], s1l[1:2, :] = merged(s1b)
    pltpu.make_async_copy(s1l, s2b.at[q, y], s2_r.at[0]).start()
    lax.fori_loop(1, 16, s2_start, 0)
    lax.fori_loop(3, 6, slope, 0)

    drain(two, y_s.at[2])
    z_o.wait_recv()
    o_g[0].start()
    o_g[1].start()
    drain(two, y_r.at[2])
    qf[0:8] = hb[A, rows_of(y), :].astype(F32) + ry[3].astype(F32) + ry[4].astype(F32)
    drain(two, y_r.at[3])
    qf[8:16] = hb[B, rows_of(y), :].astype(F32) + ry[2].astype(F32) + ry[5].astype(F32)
    for i in range(4):
        a2s[:, i] = qf[:, 4 * i : 4 * i + 4, :].astype(BF16)

    def a_start(cd, t):
        remote(a2s.at[cd, t], a2r.at[c * 4 + q], a_s.at[0], a_r.at[0], (cd, y * 4 + t)).start()

    pltpu.make_async_copy(a2s.at[c, q], a2r.at[c * 4 + q], a_r.at[0]).start()
    to_plane(a_start)

    loads[7].wait()
    pltpu.make_async_copy(s2b, s2b, s2_r.at[0]).wait()

    def xc_copy(i, k):
        return remote(xp.at[k, :, other], xrp.at[k], xc_s.at[0], xc_r.at[0], mate)

    def disp(i, carry):
        k = (y + 2 + i) % 4
        top, total = merged(s2b.at[k])
        d = jnp.exp(lgp[k].astype(F32) - top) * (1.0 / total)
        dspf[k] = d
        lw[k, :, 0:256] = d.astype(BF16)
        xp[k] = lax.dot_general(lw[k, :, 0:256], tok[...], TN, preferred_element_type=F32).astype(BF16)
        xc_copy(i, k).start()
        return carry

    lax.fori_loop(0, 4, disp, 0)

    obf = ob.reshape(16, 64, 768)
    drain(obf.at[pl.ds(0, 4)], o_r.at[1])
    o_g[2].start()
    o_g[3].start()

    def x_half(i, carry):
        k = (y + 2 + i) % 4
        hx[k] = (xp[k, :, mine].astype(F32) + xrp[k].astype(F32)).astype(BF16)
        return carry

    drain(xrp, xc_r.at[0])
    lax.fori_loop(0, 4, x_half, 0)
    XA, XB = pl.ds(0, 128), pl.ds(128, 128)

    def x_copy(i, src, dev):
        return remote(src, xry.at[i], x_s.at[0], x_r.at[i // 2 if i < 2 else 1], dev)

    xs = [
        x_copy(0, hx.at[y2, XA], right),
        x_copy(1, hx.at[y2, XB], left),
        x_copy(2, hx.at[yr, XB], right),
        x_copy(3, hx.at[yl, XA], left),
        x_copy(4, xst.at[0], right),
        x_copy(5, xst.at[1], left),
    ]
    xs[0].start()
    xs[1].start()
    drain(ptf.at[pl.ds(0, 16)], p_r.at[2])
    ps[6].start()
    ps[7].start()

    loads[6].wait()
    pltpu.make_async_copy(a2r, a2r, a_r.at[0]).wait()
    for i in range(16):
        for j in range(2):
            xf[4 * i : 4 * i + 4, 384 * j : 384 * j + 384] = (
                a2r[4 * i + j].astype(F32) + a2r[4 * i + 2 + j].astype(F32)
            )
    x_b = xf[...].astype(BF16)

    def act(i, carry):
        part = pl.ds(pl.multiple_of(i * 1024, 1024), 1024)
        a = lax.dot_general(x_b, wout[part, :], NT, preferred_element_type=F32)
        hc[:, part] = (a * gp[:, part]).astype(BF16)
        return carry

    lax.fori_loop(0, 3, act, 0)
    xs[2].start()
    xs[3].start()

    def grad(i, carry):
        part = pl.ds(pl.multiple_of(i * 256, 256), 256)
        xf[:, part] = lax.dot_general(hc[...], win[part, :], NT, preferred_element_type=F32)
        return carry

    lax.fori_loop(0, 3, grad, 0)
    for i in range(16):
        for j in range(2):
            b2s[i, j] = xf[4 * i : 4 * i + 4, 384 * j : 384 * j + 384].astype(BF16)

    def b_start(cd, t):
        remote(b2s.at[cd, t % 2], b2r.at[c * 4 + q], b_s.at[0], b_r.at[0], (cd, y * 4 + t)).start()

    pltpu.make_async_copy(b2s.at[c, h], b2r.at[c * 4 + q], b_r.at[0]).start()
    to_plane(b_start)

    drain(obf.at[pl.ds(0, 2)], o_r.at[2])
    o_g[4].start()
    drain(two, x_r.at[0])
    xst[0] = (xry[0].astype(F32) + hx[yr, XA, :].astype(F32)).astype(BF16)
    xs[4].start()
    xst[1] = (xry[1].astype(F32) + hx[yl, XB, :].astype(F32)).astype(BF16)
    xs[5].start()
    drain(ptf.at[pl.ds(0, 8)], p_r.at[3])
    ps[8].start()
    o_g[4].wait_recv()

    def comb_dot(i, carry):
        cols = pl.ds(pl.multiple_of(i * 256, 256), 256)
        w = ob[i].reshape(256, 768)
        cc[:, cols] = lax.dot_general(og[...], w, NT, preferred_element_type=F32)
        return carry

    lax.fori_loop(0, 4, comb_dot, 0)

    def comb_grad(i, carry):
        rows = pl.ds(pl.multiple_of(i * 64, 64), 64)
        comb = cf[rows, :]
        v = cc[rows, :]
        cb[rows, :] = (comb * (v - jnp.sum(comb * v, axis=1, keepdims=True))).astype(BF16)
        return carry

    lax.fori_loop(0, 8, comb_grad, 0)
    ps[8].wait_recv()

    def comb_out(i, carry):
        cols = pl.ds(pl.multiple_of(i * 256, 256), 256)
        w = sp[1, :, :, cols].reshape(1024, 256)
        acc[:, cols] = jnp.dot(cb[...], w, preferred_element_type=F32)
        return carry

    lax.fori_loop(0, 3, comb_out, 0)
    drain(rp.at[pl.ds(0, 8)], x_r.at[1])
    xq[XA, :] = hx[y, XA, :].astype(F32) + xry[3].astype(F32) + xry[4].astype(F32)
    xq[XB, :] = hx[y, XB, :].astype(F32) + xry[2].astype(F32) + xry[5].astype(F32)

    pltpu.make_async_copy(b2r, b2r, b_r.at[0]).wait()
    back = b2r[...].reshape(16, 4, 4, 384)
    for i in range(4):
        zf[:, 4 * i : 4 * i + 4, :] = back[:, i].astype(F32)
    sgb[:, rows_of(y), mine] = zf[...].astype(BF16)

    def g_copy(i, part, yy, dev):
        ref = sgb.at[part, rows_of(yy), mine]
        return remote(ref, ref, g_s.at[min(i // 2, 1)], g_r.at[(0, 1, 2, 2, 3, 3)[i]], dev)

    def k_copy(i, part, yy):
        ref = sgb.at[part, rows_of(yy), mine]
        return remote(ref, ref, k_s.at[0], k_r.at[(0, 0, 1, 2, 1, 2, 3, 3)[i]], mate)

    gs = [
        g_copy(0, A, y, right),
        g_copy(1, B, y, left),
        g_copy(2, B, y, right),
        g_copy(3, A, y, left),
        g_copy(4, A, yl, right),
        g_copy(5, B, yr, left),
    ]
    ks = [
        k_copy(0, A, y),
        k_copy(1, B, y),
        k_copy(2, A, yl),
        k_copy(3, B, yr),
        k_copy(4, B, yl),
        k_copy(5, A, yr),
        k_copy(6, A, y2),
        k_copy(7, B, y2),
    ]
    gs[0].start()
    gs[1].start()
    ks[0].start()
    ks[1].start()

    prod = zf[...].reshape(256, 384) * xq[...]
    ones = jnp.ones((8, 384), F32)
    dots = lax.dot_general(ones, prod, NT, precision=lax.Precision.HIGHEST, preferred_element_type=F32)
    dtl[...] = dots[0:1, :]

    def dt_copy(i):
        return remote(dtl, dtb.at[s], dt_s.at[0], dt_r.at[0], group(i))

    pltpu.make_async_copy(dtl, dtb.at[s], dt_r.at[0]).start()

    def dt_start(i, carry):
        dt_copy(i).start()
        return carry

    lax.fori_loop(1, 16, dt_start, 0)
    drain(two, g_s.at[0])
    gs[2].start()
    gs[3].start()
    gs[0].wait_recv()
    gs[4].start()
    ks[2].start()
    gs[1].wait_recv()
    gs[5].start()
    ks[3].start()
    pltpu.make_async_copy(dtb, dtb, dt_r.at[0]).wait()

    def columns(yy, half):
        w = sgb[:, rows_of(yy), half].reshape(256, 384)
        return lax.dot_general(tok[:, half], w, NT, preferred_element_type=F32)

    def prepare(yy, begun=None):
        if begun is None:
            w = sgb[:, rows_of(yy), :].reshape(256, 768)
            d = lax.dot_general(tok[...], w, NT, preferred_element_type=F32)
        else:
            d = begun[...] + columns(yy, other)
        lw[yy, :, 256:512] = (dspf[yy] * (d - jnp.sum(dtb[pl.ds(yy * 4, 4)], axis=0))).astype(BF16)

    def use(yy):
        return jnp.dot(lw[yy], sp[:, :, rows_of(yy), :].reshape(512, 768), preferred_element_type=F32)

    drain(two, k_r.at[0])
    prepare(y)
    acc[...] += use(y)
    drain(two, g_r.at[2])
    ks[4].start()
    ks[5].start()
    dn[0] = columns(yl, mine)
    dn[1] = columns(yr, mine)
    drain(two, k_r.at[1])
    prepare(yl, dn.at[0])
    drain(two, k_r.at[2])
    prepare(yr, dn.at[1])
    drain(two, g_r.at[3])
    ks[6].start()
    ks[7].start()
    acc[...] += use(yl)
    acc[...] += use(yr)
    drain(two, k_r.at[3])
    prepare(y2)
    out_ref[0] = (acc[...] + use(y2)).astype(BF16)

    drain(two, y_s.at[1])
    drain(obf.at[pl.ds(0, 15)], o_s.at[0])
    drain(ptf.at[pl.ds(0, 63)], p_s.at[0])
    drain(rp, cs_s.at[0])
    drain(rp, xc_s.at[0])
    drain(rp, k_s.at[0])
    drain(rp.at[pl.ds(0, 12)], x_s.at[0])
    drain(rp.at[pl.ds(0, 8)], g_s.at[1])
    drain(a2r.at[pl.ds(0, 63)], a_s.at[0])
    drain(b2r.at[pl.ds(0, 63)], b_s.at[0])
    drain(s1b.at[pl.ds(0, 3)], s1_s.at[0])
    drain(s2b.reshape(16, 2, 256).at[pl.ds(0, 15)], s2_s.at[0])
    drain(dtb.at[pl.ds(0, 15)], dt_s.at[0])


def on_device(tokens, out_grad, saved_logits, slot_params, slot_inputs, slot_outputs, expert_in, expert_out):
    any_spec = pl.BlockSpec(memory_space=pl.ANY)
    vm = pltpu.VMEM
    dma = pltpu.SemaphoreType.DMA
    return pl.pallas_call(
        kernel,
        out_shape=pltpu.VMEM((1, 512, 768), BF16),
        in_specs=[any_spec] * 8,
        out_specs=pl.BlockSpec(memory_space=pltpu.VMEM),
        scratch_shapes=[
            vm((512, 1024), BF16),
            vm((512, 768), BF16),
            vm((512, 768), BF16),
            vm((768, 3072), BF16),
            vm((3072, 768), BF16),
            vm((16, 4, 768), BF16),
            vm((512, 1024), F32),
            vm((512, 1024), BF16),
            vm((16, 64, 768), BF16),
            vm((16, 64, 384), BF16),
            vm((16, 64, 384), BF16),
            vm((6, 8, 16, 384), BF16),
            vm((2, 8, 16, 384), BF16),
            vm((16, 16, 384), F32),
            vm((16, 4, 4, 384), BF16),
            vm((64, 4, 384), BF16),
            vm((64, 768), F32),
            vm((64, 3072), F32),
            vm((64, 3072), BF16),
            vm((16, 2, 4, 384), BF16),
            vm((64, 4, 384), BF16),
            vm((16, 16, 384), F32),
            vm((2, 16, 64, 768), BF16),
            vm((4, 2, 2, 64, 768), BF16),
            vm((512, 1024), F32),
            vm((4, 512, 256), F32),
            vm((4, 512, 512), BF16),
            vm((4, 2, 256), F32),
            vm((4, 2, 256), F32),
            vm((2, 256), F32),
            vm((4, 4, 2, 256), F32),
            vm((1, 256), F32),
            vm((16, 1, 256), F32),
            vm((512, 768), F32),
            vm((4, 512, 256), BF16),
            vm((4, 256, 768), BF16),
            vm((4, 256, 384), BF16),
            vm((4, 256, 384), BF16),
            vm((6, 128, 384), BF16),
            vm((2, 128, 384), BF16),
            vm((256, 384), F32),
            vm((2, 512, 256), F32),
            dma((2,)), dma((7,)),
            dma((1,)), dma((4,)),
            dma((3,)), dma((4,)),
            dma((1,)), dma((1,)),
            dma((1,)), dma((1,)),
            dma((2,)), dma((4,)),
            dma((1,)), dma((4,)),
            dma((1,)), dma((4,)),
            dma((1,)), dma((5,)),
            dma((1,)), dma((1,)),
            dma((1,)), dma((1,)),
            dma((1,)), dma((1,)),
            dma((1,)), dma((1,)),
            dma((1,)), dma((2,)),
        ],
        compiler_params=pltpu.CompilerParams(
            collective_id=0, has_side_effects=True, vmem_limit_bytes=60 * 1024 * 1024
        ),
    )(tokens, out_grad, saved_logits, slot_params.T, slot_inputs, slot_outputs, expert_in, expert_out)


def solution(mesh):
    placed = (
        P("clip", "seq", None),
        P("clip", "seq", None),
        P("clip", "seq", None),
        P(None, "seq"),
        P(None, ("clip", "seq"), None),
        P("clip", "seq", None),
        P(("clip", "seq"), None, None),
        P(("clip", "seq"), None, None),
    )
    return jax.shard_map(
        on_device, mesh=mesh, in_specs=placed, out_specs=P("clip", "seq", None), check_vma=False
    )
```
